128 devices in a mesh: dev: 128 (over x, y, z, core).
Axes of the slice: x: 4, y: 4, z: 4, core: 2. Of those that a mesh axis runs over, the one named last changes fastest.
Arguments:
- peripheral: bfloat16 [524288, 256], P('dev'), may hold values from -6 to 6
- hubs: bfloat16 [2048, 256], P('dev'), may hold values from -6 to 6
- tiles: bfloat16 [55296, 128, 128], P('dev'), may hold values from -0.25 to 0.25
- tile_rows: int32 [55296], P('dev'), may hold values from 0 to 4111, as said below
- local_cols: int32 [38912], P('dev'), may hold values from 0 to 4111, as said below
- tile_count: int32 [128], P('dev'), may hold values from 128 to 432, as said below
- send_list: int32 [128, 128], P('dev'), may hold values from 0 to 31
- hub_place: int32 [2048], replicated, may hold values from 0 to 2047, each once
- w_in: bfloat16 [2, 256, 2048], replicated, may hold values from -0.375 to 0.375
- w_out: bfloat16 [2, 2048, 256], replicated, may hold values from -0.125 to 0.125
Outputs:
- peripheral_out: bfloat16 [524288, 256], P('dev')
- hubs_out: bfloat16 [2048, 256], P('dev')
The draws below stay inside these ranges and needn't reach their ends.
Inputs may be any that keep to these rules, and one draw needn't show every extreme that they name: `tile_rows`: row blocks of device d's slots are hub blocks (below 16) or d's own blocks 16 + d * 32 to 16 + d * 32 + 31; slots below 128 always name an own block. `local_cols`: column blocks of device d's slots from 128 on are hub blocks or d's own blocks. `tile_count`: every device holds at least 128 live slots; some device is full in every draw.
All inputs are finite; a program needn't handle non-finite values.
Results may differ from the reference program's by a relative error of at most 0.005.
Values may be sent and summed in bfloat16 or wider, within the bound.
A program may use at most 128 MiB of HBM per device.

```python
import jax
import jax.numpy as jnp
from jax import lax

F = 256
FF = 2048
BLK = 128
HB = 16
LAYERS = 2
PB = 32
EX = 16
NDEV = 128
H = 2048
CAP = 432
PDEV = 4096
PERI = 524288


def graph_plan(key):
    keys = [jax.random.fold_in(key, 101 + number) for number in range(10)]
    sending = jax.random.randint(keys[0], (NDEV, NDEV), 0, PB, dtype=jnp.int32)
    device_ids = jnp.arange(NDEV, dtype=jnp.int32)[:, None]
    slot_index = jnp.arange(CAP, dtype=jnp.int32)[None, :]
    own_row = jax.random.randint(keys[1], (NDEV, CAP), 0, PB, dtype=jnp.int32)
    hub_row = jax.random.randint(keys[2], (NDEV, CAP), 0, HB, dtype=jnp.int32)
    pick_row = jax.random.randint(keys[3], (NDEV, CAP), 0, 2, dtype=jnp.int32)
    rows_all = jnp.where((slot_index >= NDEV) & (pick_row == 0), hub_row, HB + device_ids * PB + own_row)
    own_col = jax.random.randint(keys[4], (NDEV, CAP - NDEV), 0, PB, dtype=jnp.int32)
    hub_col = jax.random.randint(keys[5], (NDEV, CAP - NDEV), 0, HB, dtype=jnp.int32)
    pick_col = jax.random.randint(keys[6], (NDEV, CAP - NDEV), 0, 2, dtype=jnp.int32)
    cols_all = jnp.where(pick_col == 0, hub_col, HB + device_ids * PB + own_col)
    base_count = NDEV + jax.random.randint(keys[7], (NDEV,), 0, 2 * EX + 1, dtype=jnp.int32)
    forced = jax.random.randint(keys[8], (), 0, NDEV, dtype=jnp.int32)
    heavy = (jax.random.randint(keys[9], (NDEV,), 0, 8, dtype=jnp.int32) == 0) | (jnp.arange(NDEV, dtype=jnp.int32) == forced)
    counts = jnp.where(heavy, CAP, base_count).astype(jnp.int32)
    return (sending, rows_all.reshape(-1).astype(jnp.int32), cols_all.reshape(-1).astype(jnp.int32), counts)


def draw_tile_rows(key, part):
    return graph_plan(key)[1]


def draw_local_cols(key, part):
    return graph_plan(key)[2]


def draw_tile_count(key, part):
    return graph_plan(key)[3]


def draw_send_list(key, part):
    return graph_plan(key)[0]


def steps_of(key, dims, pieces, least, top_value):
    def one(dim, shards_of):
        draws = jax.random.uniform(jax.random.fold_in(jax.random.fold_in(key, 6), dim), (shards_of,), jnp.float32, least / len(pieces), top_value / len(pieces))
        return jnp.repeat(jnp.exp(draws), dims[dim] // shards_of).reshape((-1,) + (1,) * (len(dims) - dim - 1))

    level = one(*pieces[0])
    for cut in pieces[1:]:
        level = level * one(*cut)
    return level


def centred(stream_key, shape, spread, bound, pieces=(), kind=jnp.bfloat16):
    array = jax.random.normal(stream_key, shape, jnp.float32) * spread
    if len(pieces) > 0:
        array = steps_of(stream_key, shape, pieces, -0.22, 0.18) * array
    return jnp.clip(array, min=-bound, max=bound).astype(kind)


def setup_inputs(seed: int = 0) -> dict:
    key_list = jax.random.split(jax.random.key(seed), 11)
    peripheral = centred(key_list[0], (PERI, F), 1.0, 6.0, ((0, 128),))
    hubs = centred(key_list[1], (H, F), 1.0, 6.0, ((0, 128),))
    tiles = centred(key_list[2], (NDEV * CAP, BLK, BLK), (BLK * NDEV // PB) ** -0.5, 0.25, ((0, 128),))
    tile_rows = draw_tile_rows(jax.random.fold_in(key_list[10], 71), 0)
    local_cols = draw_local_cols(jax.random.fold_in(key_list[10], 71), 0)
    tile_count = draw_tile_count(jax.random.fold_in(key_list[10], 71), 0)
    send_list = draw_send_list(jax.random.fold_in(key_list[10], 71), 0)
    hub_place = jax.random.permutation(key_list[7], H).astype(jnp.int32)
    w_in = centred(key_list[8], (LAYERS, F, FF), F ** -0.5, 0.375)
    w_out = centred(key_list[9], (LAYERS, FF, F), FF ** -0.5, 0.125)
    return {"peripheral": peripheral, "hubs": hubs, "tiles": tiles, "tile_rows": tile_rows, "local_cols": local_cols, "tile_count": tile_count, "send_list": send_list, "hub_place": hub_place, "w_in": w_in, "w_out": w_out}


epsilon = 1e-06

def feed_forward(rows_in, summed, first, second):
    united = rows_in.astype(jnp.float32) + summed
    normed = (united * lax.rsqrt(lax.optimization_barrier(jnp.mean(united * united, axis=-1, keepdims=True)) + epsilon)).astype(jnp.bfloat16)
    hidden = jnp.maximum(jnp.dot(normed, first, preferred_element_type=jnp.float32), 0.0).astype(jnp.bfloat16)
    return (united + jnp.dot(hidden, second, preferred_element_type=jnp.float32)).astype(jnp.bfloat16)

def reference(peripheral, hubs, tiles, tile_rows, local_cols, tile_count, send_list, hub_place, w_in, w_out):
    devices = NDEV
    remote_cols = HB + jnp.arange(devices, dtype=jnp.int32)[None, :] * PB + send_list.T.astype(jnp.int32)
    columns = jnp.concatenate([remote_cols, local_cols.reshape(devices, CAP - devices).astype(jnp.int32)], axis=1)
    rows_all = tile_rows.reshape(devices, CAP).astype(jnp.int32)
    live_slot = (jnp.arange(CAP, dtype=jnp.int32)[None, :] < tile_count[:, None]).astype(jnp.float32)
    tiles_dev = tiles.reshape(devices, CAP, BLK, BLK)
    inverse = jnp.argsort(hub_place).astype(jnp.int32)
    peri_rows, hub_rows = (peripheral, hubs)
    for layer_index in range(LAYERS):
        column_table = jnp.concatenate([hub_rows[hub_place].reshape(HB, BLK, F), peri_rows.reshape(devices * PB, BLK, F)], axis=0)

        def device_step(total, items):
            tile_block, row_block, col_block, live = items
            products = jnp.einsum('tij,tjf->tif', tile_block.astype(jnp.float32), column_table[col_block].astype(jnp.float32), precision=lax.Precision.HIGHEST)
            return (total.at[row_block].add(products * live[:, None, None]), None)
        start = jnp.zeros((HB + devices * PB, BLK, F), jnp.float32)
        summed, unused = lax.scan(device_step, start, (tiles_dev, rows_all, columns, live_slot))
        hub_sum = summed[:HB].reshape(H, F)[inverse]
        peri_sum = summed[HB:].reshape(devices, PDEV, F)
        first, second = (w_in[layer_index], w_out[layer_index])
        new_peri = lax.map(lambda pair: feed_forward(pair[0], pair[1], first, second), (peri_rows.reshape(devices, PDEV, F), peri_sum))
        hub_rows = feed_forward(hub_rows, hub_sum, first, second)
        peri_rows = new_peri.reshape(devices * PDEV, F)
    return (peri_rows, hub_rows)
```

```python
import functools
import jax
import jax.numpy as jnp
from jax import lax
from jax.sharding import PartitionSpec as P
from jax.experimental import pallas as pl
from jax.experimental.pallas import tpu as pltpu

MESH = pl.DeviceIdType.MESH
ROWS = ((0, 48), (48, 48), (96, 32))
CH = 4
epsilon = 1e-06


def coords():
    me = lax.axis_index("dev")
    return [me // 32, lax.rem(me // 8, 4), lax.rem(me // 2, 4)], lax.rem(me, 2)


def device_of(co, core):
    return ((co[0] * 4 + co[1]) * 4 + co[2]) * 2 + core


def moved(co, dim, off):
    out = list(co)
    out[dim] = lax.rem(co[dim] + off, 4)
    return out


def exchange_kernel(permute, x_ref, list_ref, hub_ref, place_ref, in_ref, near_ref, hubs_ref,
                    lists, gathered, wide, ordered, t00, t01, t02, t10, t11, t12, t20, t21, t22, s0, s1, s2, r0, r1, r2,
                    list_sem, list_send, smem_sem, ag_send, ag_recv, p2_send, p2_recv, p3_send, p3_recv, local_sem, hub_send, hub_recv):
    tabs = ((t00, t01, t02), (t10, t11, t12), (t20, t21, t22))
    stage, relay = (s0, s1, s2), (r0, r1, r2)
    co, core = coords()
    blocks = x_ref.shape[0]
    per = blocks // CH

    def to(co2, core2):
        return (device_of(co2, core2),)

    bar = pltpu.get_barrier_semaphore()
    for dim in range(3):
        for off in (1, 2, 3):
            for flip in (0, 1):
                pl.semaphore_signal(bar, inc=1, device_id=to(moved(co, dim, off), lax.rem(core + flip, 2)), device_id_type=MESH)
    pl.semaphore_signal(bar, inc=1, device_id=to(co, 1 - core), device_id_type=MESH)
    pl.semaphore_wait(bar, 19)

    def remote(src, dst, ssem, rsem, dev):
        return pltpu.make_async_remote_copy(src_ref=src, dst_ref=dst, send_sem=ssem, recv_sem=rsem, device_id=dev, device_id_type=MESH)

    def list_copy(dim, off):
        return remote(list_ref, near_ref.at[pl.ds(dim * 4 + 4 - off, 1)], list_send.at[dim, off], list_sem.at[dim, 4 - off], to(moved(co, dim, off), core))

    for dim in range(3):
        for off in (1, 2, 3):
            list_copy(dim, off).start()

    def hub_copy(step, off):
        if step == 3:
            part = gathered.at[:, :, :, core]
            return remote(part, part, hub_send.at[3, 0], hub_recv.at[3, 0], to(co, 1 - core))
        dim = 2 - step
        part = (gathered.at[co[0], co[1], co[2], core], gathered.at[co[0], co[1], :, core], gathered.at[co[0], :, :, core])[step]
        return remote(part, part, hub_send.at[step, off - 1], hub_recv.at[step, 3 - off], to(moved(co, dim, off), core))

    hub_own = pltpu.make_async_copy(hub_ref, gathered.at[co[0], co[1], co[2], core], local_sem.at[1])
    hub_own.start()
    hub_own.wait()

    def hub_start(step):
        for off in (1, 2, 3) if step < 3 else (1,):
            hub_copy(step, off).start()

    def hub_wait(step):
        for off in (1, 2, 3) if step < 3 else (1,):
            hub_copy(step, off).wait()

    hub_start(0)

    def ag_copy(p, q, direction):
        lo, n = ROWS[p]
        off = 1 if direction == 0 else 3
        seen = 4 - off
        return remote(x_ref.at[pl.ds(q * per, per), pl.ds(lo, n)], tabs[p][seen - 1].at[pl.ds(q * per, per)],
                      ag_send.at[p, q, direction], ag_recv.at[p, q, seen - 1], to(moved(co, p, off), core))

    def relay_copy(p, q):
        off = 1 if q % 2 == 0 else 3
        seen = 4 - off
        return remote(tabs[p][seen - 1].at[pl.ds(q * per, per)], tabs[p][1].at[pl.ds(q * per, per)],
                      ag_send.at[p, q, 2], ag_recv.at[p, q, 1], to(moved(co, p, off), core))

    for q in range(CH):
        for p in range(3):
            for direction in ((0, 1) if q % 2 == 0 else (1, 0)):
                ag_copy(p, q, direction).start()

    own = pltpu.make_async_copy(list_ref, near_ref.at[pl.ds(0, 1)], local_sem.at[0])
    own.start()
    own.wait()
    for dim in range(3):
        for off in (1, 2, 3):
            list_copy(dim, off).wait_recv()
    fetch = pltpu.make_async_copy(near_ref, lists, smem_sem)
    fetch.start()
    fetch.wait()

    def assemble(p, i, js):
        lo, n = ROWS[p]
        d1, d2 = (p + 1) % 3, (p + 2) % 3
        where = lax.rem(co[p] + i, 4)
        row = 0 if i == 0 else p * 4 + i
        for j in js:
            def piece(m, carry, j=j):
                k, flip = m // 2, lax.rem(m, 2)
                target = device_of(moved(moved(co, d1, j), d2, k), flip)
                b = lists[row, target]
                value = x_ref[b, lo:lo + n, :] if i == 0 else tabs[p][i - 1][b]
                stage[p][j, k, flip, where] = value
                return carry
            lax.fori_loop(0, 8, piece, 0)

    def p2_copy(p, i, j):
        d1 = (p + 1) % 3
        where = lax.rem(co[p] + i, 4)
        return remote(stage[p].at[j, :, :, where], relay[p].at[3 - j, :, :, where],
                      p2_send.at[p, i, j - 1], p2_recv.at[p, i, 3 - j], to(moved(co, d1, j), core))

    def send2(p, i):
        for j in (1, 3, 2):
            p2_copy(p, i, j).start()

    for p in range(3):
        assemble(p, 0, (1, 3, 2, 0))
    hub_wait(0)
    hub_start(1)
    for p in range(3):
        send2(p, 0)
    for q in range(CH):
        for p in range(3):
            seen = 3 if q % 2 == 0 else 1
            ag_wait(ag_recv, tabs, p, q, seen - 1, per)
            relay_copy(p, q).start()
    hub_wait(1)
    hub_start(2)
    for i in (1, 3, 2):
        if i == 2:
            hub_wait(2)
            hub_start(3)
        for p in range(3):
            for q in range(CH):
                if i == 2 or (i == 1 and q % 2 == 0) or (i == 3 and q % 2 == 1):
                    ag_wait(ag_recv, tabs, p, q, i - 1, per)
            assemble(p, i, (1, 3, 2, 0))
        for p in range(3):
            send2(p, i)

    place = ((0, 1, 2), (2, 0, 1), (1, 2, 0))

    def landing(p, s1, s2, s_core):
        lo, n = ROWS[p]
        idx = [None, None, None]
        idx[p] = slice(None)
        idx[(p + 1) % 3] = s1
        idx[(p + 2) % 3] = s2
        return in_ref.at[idx[0], idx[1], idx[2], s_core, pl.ds(lo, n)]

    def p3_copy(p, j, k, flip):
        d1, d2 = (p + 1) % 3, (p + 2) % 3
        src = stage[p].at[0, k, lax.rem(core + flip, 2)] if j == 0 else relay[p].at[j - 1, k, lax.rem(core + flip, 2)]
        s1 = lax.rem(co[d1] + j, 4)
        dst = landing(p, s1, co[d2], core)
        if k == 0 and flip == 0:
            return pltpu.make_async_copy(src, dst, local_sem.at[p * 4 + j])
        return remote(src, dst, p3_send.at[p, j, k * 2 + flip], p3_recv.at[p, j, k * 2 + flip], to(moved(co, d2, k), lax.rem(core + flip, 2)))

    def send3(p, j):
        for k in (1, 3, 2, 0):
            for flip in (0, 1):
                p3_copy(p, j, k, flip).start()

    for p in range(3):
        send3(p, 0)
    for j in (1, 3, 2):
        for p in range(3):
            for i in range(4):
                p2_wait(p2_recv, relay, p, i, j - 1)
            send3(p, j)
    hub_wait(3)
    if permute:
        wide[...] = gathered[...].astype(jnp.float32).reshape(wide.shape)

        def rows8(g, carry):
            for r in range(8):
                ordered[pl.ds(g * 8 + r, 1), :] = wide[pl.ds(place_ref[g * 8 + r], 1), :]
            return carry

        lax.fori_loop(0, wide.shape[0] // 8, rows8, 0)
        hubs_ref[...] = ordered[...].astype(jnp.bfloat16)
    else:
        hubs_ref[...] = gathered[...].reshape(hubs_ref.shape)
    for p in range(3):
        for j in range(4):
            for k in range(4):
                for flip in (0, 1):
                    if k == 0 and flip == 0:
                        p3_copy(p, j, k, flip).wait()
                    else:
                        p3_copy(p, j, k, flip).wait()
    for p in range(3):
        for q in range(CH):
            ag_copy(p, q, 0).wait_send()
            ag_copy(p, q, 1).wait_send()
            relay_copy(p, q).wait_send()
        for i in range(4):
            for j in (1, 2, 3):
                p2_copy(p, i, j).wait_send()
    for dim in range(3):
        for off in (1, 2, 3):
            list_copy(dim, off).wait_send()


def ag_wait(sem, tabs, p, q, slot, per):
    ref = tabs[p][slot].at[pl.ds(q * per, per)]
    pltpu.make_async_copy(ref, ref, sem.at[p, q, slot]).wait()


def p2_wait(sem, relay, p, i, slot):
    ref = relay[p].at[slot, :, :, 0]
    pltpu.make_async_copy(ref, ref, sem.at[p, i, slot]).wait()


def exchange(x, send_list, hubs, place, permute, cid):
    bf = jnp.bfloat16
    blocks = x.shape[0]
    hub_rows = place.shape[0]
    f32 = jnp.float32
    scratch = [pltpu.SMEM((12, 128), jnp.int32), pltpu.VMEM((4, 4, 4, 2, 16, 256), bf)]
    scratch += [pltpu.VMEM((hub_rows if permute else 8, 256), f32) for _ in range(2)]
    scratch += [pltpu.VMEM((blocks, n, 256), bf) for lo, n in ROWS for _ in range(3)]
    scratch += [pltpu.VMEM((4, 4, 2, 4, n, 256), bf) for lo, n in ROWS]
    scratch += [pltpu.VMEM((3, 4, 2, 4, n, 256), bf) for lo, n in ROWS]
    D = pltpu.SemaphoreType.DMA
    scratch += [D((3, 4)), D((3, 4)), D, D((3, CH, 3)), D((3, CH, 3)), D((3, 4, 3)), D((3, 4, 3)), D((3, 4, 8)), D((3, 4, 8)), D((12,))]
    scratch += [D((4, 3)), D((4, 3))]
    V = pl.BlockSpec(memory_space=pltpu.VMEM)
    landed, near, table = pl.pallas_call(
        functools.partial(exchange_kernel, permute),
        out_shape=(
            jax.ShapeDtypeStruct((4, 4, 4, 2, 128, 256), bf),
            jax.ShapeDtypeStruct((12, 128), jnp.int32),
            jax.ShapeDtypeStruct((hub_rows, 256), bf),
        ),
        in_specs=[V, V, V, pl.BlockSpec(memory_space=pltpu.SMEM)],
        out_specs=(pl.BlockSpec(memory_space=pltpu.HBM), V, V),
        scratch_shapes=scratch,
        compiler_params=pltpu.CompilerParams(collective_id=cid, has_side_effects=True, vmem_limit_bytes=60 * 2**20),
        name="exchange",
    )(x, send_list, hubs, place)
    return landed, table


GROUP = 16


def tiles_kernel(last, rows_ref, cols_ref, count_ref, place_ref, tiles_ref, x_ref, hubs_ref, in_ref, out_ref, *rest):
    group = pl.program_id(0)
    hub_count, own_count, remote_groups = 16, 32, 128 // GROUP
    table = rest[-1]
    count = count_ref[0]
    first = lax.axis_index("dev") == 0

    @pl.when(group == 0)
    def _():
        hub = hubs_ref[...].astype(jnp.float32)
        out_ref[0:hub_count] = jnp.where(first, hub, 0.0)
        table[0:hub_count] = hubs_ref[...]

        def own(b, carry):
            block = x_ref[b]
            out_ref[hub_count + b] = block.astype(jnp.float32)
            table[hub_count + b] = block
            return carry

        lax.fori_loop(0, own_count, own, 0)

    def add(slot, tile, block):
        row = rows_ref[slot]
        out_ref[row] = out_ref[row] + jnp.dot(tile, block, preferred_element_type=jnp.float32)

    live = jnp.clip(count - group * GROUP, 0, GROUP)

    @pl.when(group < remote_groups)
    def _():
        def step(t, carry):
            for s in range(4):
                add(group * GROUP + t * 4 + s, tiles_ref[t * 4 + s], in_ref[t * 4 + s])
            return carry

        lax.fori_loop(0, GROUP // 4, step, 0)

    def local(s):
        slot = group * GROUP + s
        add(slot, tiles_ref[s], table[cols_ref[slot - 128]])

    @pl.when((group >= remote_groups) & (live == GROUP))
    def _():
        def step(t, carry):
            for s in range(4):
                local(t * 4 + s)
            return carry

        lax.fori_loop(0, GROUP // 4, step, 0)

    @pl.when((group >= remote_groups) & (live < GROUP))
    def _():
        lax.fori_loop(0, live, lambda s, carry: (local(s), carry)[1], 0)

    if last:
        perm_ref = rest[0]

        @pl.when(group == pl.num_programs(0) - 1)
        def _():
            def rows8(g, carry):
                block = out_ref[g // 16, pl.ds(lax.rem(g, 16) * 8, 8), :]
                for r in range(8):
                    perm_ref[pl.ds(place_ref[g * 8 + r], 1), :] = block[r : r + 1]
                return carry

            lax.fori_loop(0, place_ref.shape[0] // 8, rows8, 0)


def sum_tiles(last, rows, cols, count, place, tiles, x, hubs, landed):
    capacity = tiles.shape[0]
    f32 = jnp.float32
    groups = capacity // GROUP

    def full(*shape):
        return pl.BlockSpec(shape, lambda g, *s: (0,) * len(shape))

    out_shape = [jax.ShapeDtypeStruct((48, 128, 256), f32)]
    out_specs = [full(48, 128, 256)]
    if last:
        out_shape.append(jax.ShapeDtypeStruct((2048, 256), f32))
        out_specs.append(full(2048, 256))
    return pl.pallas_call(
        functools.partial(tiles_kernel, last),
        grid_spec=pltpu.PrefetchScalarGridSpec(
            num_scalar_prefetch=4,
            grid=(groups,),
            in_specs=[
                pl.BlockSpec((GROUP, 128, 128), lambda g, rows, cols, count, place: (jnp.minimum(g, (count[0] - 1) // GROUP), 0, 0)),
                full(32, 128, 256),
                full(16, 128, 256),
                pl.BlockSpec((GROUP, 128, 256), lambda g, *s: (jnp.minimum(g, 128 // GROUP - 1), 0, 0)),
            ],
            out_specs=out_specs,
            scratch_shapes=[pltpu.VMEM((48, 128, 256), jnp.bfloat16)],
        ),
        out_shape=out_shape,
        compiler_params=pltpu.CompilerParams(dimension_semantics=("arbitrary",), vmem_limit_bytes=60 * 2**20),
        name="sum_tiles",
    )(rows, cols, count, place, tiles, x, hubs.reshape(16, 128, 256), landed.reshape(128, 128, 256))


def feed_forward(united, first, second):
    scale = lax.rsqrt(jnp.mean(united * united, axis=-1, keepdims=True) + epsilon)
    normed = (united * scale).astype(jnp.bfloat16)
    total = united
    step = 512
    for n in range(0, first.shape[1], step):
        hidden = jnp.dot(normed, first[:, n : n + step], preferred_element_type=jnp.float32)
        hidden = jnp.maximum(hidden, 0.0).astype(jnp.bfloat16)
        total = total + jnp.dot(hidden, second[n : n + step, :], preferred_element_type=jnp.float32)
    return total.astype(jnp.bfloat16)


def update_kernel(u_ref, part_ref, first_ref, second_ref, out_ref, hub_out_ref, b0, a0, b1, a1, b2, a2, b3, send, recv):
    co, core = coords()

    def to(co2, core2):
        return (device_of(co2, core2),)

    bar = pltpu.get_barrier_semaphore()
    pl.semaphore_signal(bar, inc=1, device_id=to(co, 1 - core), device_id_type=MESH)
    for dim in range(3):
        for off in (1, 2, 3):
            pl.semaphore_signal(bar, inc=1, device_id=to(moved(co, dim, off), core), device_id_type=MESH)
    pl.semaphore_wait(bar, 10)

    def remote(src, dst, ssem, rsem, dev):
        return pltpu.make_async_remote_copy(src_ref=src, dst_ref=dst, send_sem=ssem, recv_sem=rsem, device_id=dev, device_id_type=MESH)

    held = (a0, a1, a2)
    came = (b1, b2, b3)

    def copy(step, off):
        if step == 0:
            return remote(part_ref.at[0:64, 1 - core], b0, send.at[0, 0], recv.at[0, 0], to(co, 1 - core))
        dim = step - 1
        return remote(held[dim].at[lax.rem(co[dim] + off, 4)], came[dim].at[3 - off], send.at[step, off - 1], recv.at[step, 3 - off], to(moved(co, dim, off), core))

    def start(step):
        for off in (1, 2, 3) if step else (1,):
            copy(step, off).start()

    def wait(step):
        for off in (1, 2, 3) if step else (1,):
            copy(step, off).wait()

    def ffn(i, carry):
        base = 64 + i * 16
        united = u_ref[pl.ds(base, 16)].reshape(512, 256)
        out_ref[pl.ds(i * 512, 512), :] = feed_forward(united, first_ref, second_ref)
        return carry

    start(0)
    lax.fori_loop(0, 2, ffn, 0)
    wait(0)

    def add0(i, carry):
        a0[i] = (part_ref[pl.ds(i * 16, 16), core] + b0[pl.ds(i * 16, 16)]).reshape(4, 4, 16, 256)
        return carry

    lax.fori_loop(0, 4, add0, 0)
    lax.fori_loop(2, 3, ffn, 0)
    start(1)
    lax.fori_loop(3, 5, ffn, 0)
    wait(1)
    a1[...] = a0[co[0]] + b1[0] + b1[1] + b1[2]
    lax.fori_loop(5, 6, ffn, 0)
    start(2)
    lax.fori_loop(6, 7, ffn, 0)
    wait(2)
    a2[...] = a1[co[1]] + b2[0] + b2[1] + b2[2]
    lax.fori_loop(7, 8, ffn, 0)
    start(3)
    wait(3)
    hub_out_ref[...] = feed_forward(a2[co[2]] + b3[0] + b3[1] + b3[2], first_ref, second_ref)


def update(u, part, first, second, cid):
    f32, bf = jnp.float32, jnp.bfloat16
    V = pl.BlockSpec(memory_space=pltpu.VMEM)
    D = pltpu.SemaphoreType.DMA
    W = pltpu.VMEM
    return pl.pallas_call(
        update_kernel,
        out_shape=(jax.ShapeDtypeStruct((4096, 256), bf), jax.ShapeDtypeStruct((16, 256), bf)),
        in_specs=[V] * 4,
        out_specs=(V, V),
        scratch_shapes=[
            W((64, 16, 256), f32), W((4, 4, 4, 16, 256), f32),
            W((3, 4, 4, 16, 256), f32), W((4, 4, 16, 256), f32),
            W((3, 4, 16, 256), f32), W((4, 16, 256), f32),
            W((3, 16, 256), f32), D((4, 3)), D((4, 3)),
        ],
        compiler_params=pltpu.CompilerParams(collective_id=cid, has_side_effects=True, vmem_limit_bytes=60 * 2**20),
        name="update",
    )(u.reshape(192, 2, 16, 256), part.reshape(-1, 2, 16, 256), first, second)


def body(peripheral, hubs, tiles, tile_rows, local_cols, tile_count, send_list, hub_place, w_in, w_out):
    position = lax.axis_index("dev")
    hub_count, own_count = 16, 32
    rows = jnp.where(tile_rows < hub_count, tile_rows, tile_rows - position * own_count)
    cols = jnp.where(local_cols < hub_count, local_cols, local_cols - position * own_count)
    x = peripheral.reshape(own_count, 128, 256)
    hub_own = hubs
    for layer in range(2):
        landed, table = exchange(x, send_list, hub_own, hub_place, layer == 0, 2 * layer)
        sums = sum_tiles(layer == 1, rows, cols, tile_count, hub_place, tiles, x, table, landed)
        u = sums[0]
        part = sums[1] if layer == 1 else u
        new, hub_own = update(u, part, w_in[layer], w_out[layer], 2 * layer + 1)
        x = new.reshape(own_count, 128, 256)
    return new, hub_own


def solution(mesh):
    split = P("dev")
    in_specs = (split, split, split, split, split, split, split, P(), P(), P())
    return jax.shard_map(body, mesh=mesh, in_specs=in_specs, out_specs=(split, split), check_vma=False)
```

```python
import functools
import jax
import jax.numpy as jnp
from jax import lax
from jax.sharding import PartitionSpec as P
from jax.experimental import pallas as pl
from jax.experimental.pallas import tpu as pltpu

MESH = pl.DeviceIdType.MESH
ROWS = ((0, 48), (48, 48), (96, 32))
epsilon = 1e-06


def coords():
    me = lax.axis_index("dev")
    return [me // 32, lax.rem(me // 8, 4), lax.rem(me // 2, 4)], lax.rem(me, 2)


def device_of(co, core):
    return ((co[0] * 4 + co[1]) * 4 + co[2]) * 2 + core


def moved(co, dim, off):
    out = list(co)
    out[dim] = lax.rem(co[dim] + off, 4)
    return out


def exchange_kernel(fused, CH, *refs):
    if fused:
        u_ref, lists, w1_ref, w2_ref, in_ref, hubs_ref, x_ref = refs[:7]
        first_ref, second_ref, hidden_ref, normed_ref, w_sem = refs[7:12]
        sum_refs = refs[12:23]
        refs = refs[23:]
    else:
        x_ref, list_ref, hub_ref, place_ref, in_ref, hubs_ref, near_ref, lists, wide, ordered = refs[:10]
        refs = refs[10:]
    exchange_steps(fused, CH, locals(), *refs)


def exchange_steps(fused, CH, given, gathered, t00, t01, t02, t10, t11, t12, t20, t21, t22, s0, s1, s2, r0, r1, r2,
                    list_sem, list_send, smem_sem, ag_send, ag_recv, p2_send, p2_recv, p3_send, p3_recv, local_sem, hub_send, hub_recv):
    x_ref, in_ref, hubs_ref, lists = given["x_ref"], given["in_ref"], given["hubs_ref"], given["lists"]
    if fused:
        weights = load_weights(given["w1_ref"], given["w2_ref"], given["first_ref"], given["second_ref"], given["w_sem"], 0)
    else:
        list_ref, hub_ref, place_ref, near_ref = given["list_ref"], given["hub_ref"], given["place_ref"], given["near_ref"]
    tabs = ((t00, t01, t02), (t10, t11, t12), (t20, t21, t22))
    stage, relay = (s0, s1, s2), (r0, r1, r2)
    co, core = coords()
    blocks = x_ref.shape[0]
    per = blocks // CH

    def to(co2, core2):
        return (device_of(co2, core2),)

    bar = pltpu.get_barrier_semaphore()
    for dim in range(3):
        for off in (1, 2, 3):
            for flip in (0, 1):
                pl.semaphore_signal(bar, inc=1, device_id=to(moved(co, dim, off), lax.rem(core + flip, 2)), device_id_type=MESH)
    pl.semaphore_signal(bar, inc=1, device_id=to(co, 1 - core), device_id_type=MESH)
    pl.semaphore_wait(bar, 19)

    def remote(src, dst, ssem, rsem, dev):
        return pltpu.make_async_remote_copy(src_ref=src, dst_ref=dst, send_sem=ssem, recv_sem=rsem, device_id=dev, device_id_type=MESH)

    def list_copy(dim, off):
        return remote(list_ref, near_ref.at[pl.ds(dim * 4 + 4 - off, 1)], list_send.at[dim, off], list_sem.at[dim, 4 - off], to(moved(co, dim, off), core))

    def hub_copy(step, off):
        if step == 3:
            part = gathered.at[:, :, :, core]
            return remote(part, part, hub_send.at[3, 0], hub_recv.at[3, 0], to(co, 1 - core))
        dim = 2 - step
        part = (gathered.at[co[0], co[1], co[2], core], gathered.at[co[0], co[1], :, core], gathered.at[co[0], :, :, core])[step]
        return remote(part, part, hub_send.at[step, off - 1], hub_recv.at[step, 3 - off], to(moved(co, dim, off), core))

    def hub_start(step):
        for off in (1, 2, 3) if step < 3 else (1,):
            hub_copy(step, off).start()

    def hub_wait(step):
        for off in (1, 2, 3) if step < 3 else (1,):
            hub_copy(step, off).wait()

    def ag_copy(p, q, direction):
        lo, n = ROWS[p]
        off = 1 if direction == 0 else 3
        seen = 4 - off
        return remote(x_ref.at[pl.ds(q * per, per), pl.ds(lo, n)], tabs[p][seen - 1].at[pl.ds(q * per, per)],
                      ag_send.at[p, q, direction], ag_recv.at[p, q, seen - 1], to(moved(co, p, off), core))

    def relay_copy(p, q):
        off = 1 if q % 2 == 0 else 3
        seen = 4 - off
        return remote(tabs[p][seen - 1].at[pl.ds(q * per, per)], tabs[p][1].at[pl.ds(q * per, per)],
                      ag_send.at[p, q, 2], ag_recv.at[p, q, 1], to(moved(co, p, off), core))

    def ag_start(q):
        for p in range(3):
            for direction in (0, 1) if q % 2 == 0 else (1, 0):
                ag_copy(p, q, direction).start()

    def relay_on(q):
        for p in range(3):
            ag_wait(ag_recv, tabs, p, q, 2 if q % 2 == 0 else 0, per)
            relay_copy(p, q).start()

    def assemble(p, i, js):
        lo, n = ROWS[p]
        d1, d2 = (p + 1) % 3, (p + 2) % 3
        where = lax.rem(co[p] + i, 4)
        row = 0 if i == 0 else p * 4 + i
        for j in js:
            def piece(m, carry, j=j):
                k, flip = m // 2, lax.rem(m, 2)
                target = device_of(moved(moved(co, d1, j), d2, k), flip)
                b = lists[row, target]
                value = x_ref[b, lo:lo + n, :] if i == 0 else tabs[p][i - 1][b]
                stage[p][j, k, flip, where] = value
                return carry
            lax.fori_loop(0, 8, piece, 0)

    def p2_copy(p, i, j):
        d1 = (p + 1) % 3
        where = lax.rem(co[p] + i, 4)
        return remote(stage[p].at[j, :, :, where], relay[p].at[3 - j, :, :, where],
                      p2_send.at[p, i, j - 1], p2_recv.at[p, i, 3 - j], to(moved(co, d1, j), core))

    def send2(p, i):
        for j in (1, 3, 2):
            p2_copy(p, i, j).start()

    def pass_on(i):
        for p in range(3):
            for q in range(CH):
                if i == 2 or (i == 1 and q % 2 == 0) or (i == 3 and q % 2 == 1):
                    ag_wait(ag_recv, tabs, p, q, i - 1, per)
            assemble(p, i, (1, 3, 2, 0))
            if p:
                send2(p - 1, i)
        send2(2, i)

    place = ((0, 1, 2), (2, 0, 1), (1, 2, 0))

    def landing(p, s1, s2, s_core):
        lo, n = ROWS[p]
        idx = [None, None, None]
        idx[p] = slice(None)
        idx[(p + 1) % 3] = s1
        idx[(p + 2) % 3] = s2
        return in_ref.at[idx[0], idx[1], idx[2], s_core, pl.ds(lo, n)]

    def p3_copy(p, j, k, flip):
        d1, d2 = (p + 1) % 3, (p + 2) % 3
        src = stage[p].at[0, k, lax.rem(core + flip, 2)] if j == 0 else relay[p].at[j - 1, k, lax.rem(core + flip, 2)]
        s1 = lax.rem(co[d1] + j, 4)
        dst = landing(p, s1, co[d2], core)
        if k == 0 and flip == 0:
            return pltpu.make_async_copy(src, dst, local_sem.at[p * 4 + j])
        return remote(src, dst, p3_send.at[p, j, k * 2 + flip], p3_recv.at[p, j, k * 2 + flip], to(moved(co, d2, k), lax.rem(core + flip, 2)))

    def send3(p, j):
        for k in (1, 3, 2, 0):
            for flip in (0, 1):
                p3_copy(p, j, k, flip).start()

    def finish(j):
        for p in range(3):
            for i in range(4):
                p2_wait(p2_recv, relay, p, i, j - 1)
            send3(p, j)

    def own_pass():
        for p in range(3):
            assemble(p, 0, (1, 3, 2, 0))
            if fused and p == 0:
                ag_start(CH - 1)
            if p:
                send2(p - 1, 0)
        send2(2, 0)

    if fused:
        sums = HubSum(co, core, remote, to, u_ref := given["u_ref"], *given["sum_refs"])
        sums.start(0)
        weights()
        first_ref, second_ref = given["first_ref"], given["second_ref"]
        size = 4096 // CH
        for q in range(CH):
            update_rows(u_ref, x_ref, q, size, first_ref, second_ref, given["hidden_ref"], given["normed_ref"])
            if q >= 1:
                ag_start(q - 1)
            if q == 2:
                sums.wait(0)
                sums.add(0)
            if q == 3:
                sums.start(1)
            if q >= 4:
                relay_on(q - 4)
        own_pass()
        sums.wait(1)
        sums.add(1)
        for q in range(CH - 4, CH):
            relay_on(q)
            if q == CH - 3:
                sums.start(2)
        pass_on(1)
        sums.wait(2)
        sums.add(2)
        pass_on(3)
        sums.start(3)
        pass_on(2)
        sums.wait(3)
        gathered[co[0], co[1], co[2], core] = feed_forward(sums.result(), first_ref, second_ref)
        for p in range(3):
            send3(p, 0)
        hub_start(0)
        finish(1)
        hub_wait(0)
        hub_start(1)
        finish(3)
        hub_wait(1)
        hub_start(2)
        finish(2)
        hub_wait(2)
        hub_start(3)
    else:
        for dim in range(3):
            for off in (1, 2, 3):
                list_copy(dim, off).start()
        hub_own = pltpu.make_async_copy(hub_ref, gathered.at[co[0], co[1], co[2], core], local_sem.at[1])
        hub_own.start()
        hub_own.wait()
        hub_start(0)
        for q in range(CH):
            ag_start(q)
        own = pltpu.make_async_copy(list_ref, near_ref.at[pl.ds(0, 1)], local_sem.at[0])
        own.start()
        own.wait()
        for dim in range(3):
            for off in (1, 2, 3):
                list_copy(dim, off).wait_recv()
        fetch = pltpu.make_async_copy(near_ref, lists, smem_sem)
        fetch.start()
        fetch.wait()
        own_pass()
        hub_wait(0)
        hub_start(1)
        for q in range(CH):
            relay_on(q)
        hub_wait(1)
        hub_start(2)
        pass_on(1)
        pass_on(3)
        hub_wait(2)
        hub_start(3)
        pass_on(2)
        for p in range(3):
            send3(p, 0)
        for j in (1, 3, 2):
            finish(j)
    hub_wait(3)
    if not fused:
        wide, ordered = given["wide"], given["ordered"]
        wide[...] = gathered[...].astype(jnp.float32).reshape(wide.shape)

        def rows8(g, carry):
            for r in range(8):
                ordered[pl.ds(g * 8 + r, 1), :] = wide[pl.ds(place_ref[g * 8 + r], 1), :]
            return carry

        lax.fori_loop(0, wide.shape[0] // 8, rows8, 0)
        hubs_ref[...] = ordered[...].astype(jnp.bfloat16)
    else:
        hubs_ref[...] = gathered[...].reshape(hubs_ref.shape)
    for p in range(3):
        for j in range(4):
            for k in range(4):
                for flip in (0, 1):
                    if k == 0 and flip == 0:
                        p3_copy(p, j, k, flip).wait()
                    else:
                        p3_copy(p, j, k, flip).wait()
    for p in range(3):
        for q in range(CH):
            ag_copy(p, q, 0).wait_send()
            ag_copy(p, q, 1).wait_send()
            relay_copy(p, q).wait_send()
        for i in range(4):
            for j in (1, 2, 3):
                p2_copy(p, i, j).wait_send()
    if not fused:
        for dim in range(3):
            for off in (1, 2, 3):
                list_copy(dim, off).wait_send()


def ag_wait(sem, tabs, p, q, slot, per):
    ref = tabs[p][slot].at[pl.ds(q * per, per)]
    pltpu.make_async_copy(ref, ref, sem.at[p, q, slot]).wait()


def p2_wait(sem, relay, p, i, slot):
    ref = relay[p].at[slot, :, :, 0]
    pltpu.make_async_copy(ref, ref, sem.at[p, i, slot]).wait()


def load_weights(w1_ref, w2_ref, first_ref, second_ref, sem, layer):
    copies = [
        pltpu.make_async_copy(w1_ref.at[layer], first_ref, sem.at[0]),
        pltpu.make_async_copy(w2_ref.at[layer], second_ref, sem.at[1]),
    ]
    for copy in copies:
        copy.start()

    def wait():
        for copy in copies:
            copy.wait()

    return wait


class HubSum:
    orders = ((0, 1, 2), (1, 2, 0))

    def __init__(self, co, core, remote, to, part, b0, a0, b1a, b1b, a1, b2a, b2b, a2, b3, send, recv):
        self.co, self.core, self.remote, self.to, self.part = co, core, remote, to, part
        self.b0, self.a0, self.a1, self.a2 = b0, a0, a1, a2
        self.came = ((b1a, b1b), (b2a, b2b), (b3.at[0], b3.at[1]))
        self.b3, self.send, self.recv = b3, send, recv

    def source(self, step, p, at):
        if step == 1:
            rows = pl.ds(p * 8, 8)
            return self.a0.at[at, :, :, rows] if p == 0 else self.a0.at[:, at, :, rows]
        if step == 2:
            return self.a1.at[p, at] if p == 0 else self.a1.at[p, :, at]
        return self.a2.at[p, at]

    def copies(self, step):
        if step == 0:
            return [self.remote(self.part.at[0:64, 1 - self.core], self.b0, self.send.at[0, 0, 0], self.recv.at[0, 0, 0], self.to(self.co, 1 - self.core))]
        out = []
        for p, order in enumerate(self.orders):
            dim = order[step - 1]
            for off in (1, 2, 3):
                src = self.source(step, p, lax.rem(self.co[dim] + off, 4))
                out.append(self.remote(src, self.came[step - 1][p].at[3 - off], self.send.at[step, p, off - 1], self.recv.at[step, p, 3 - off], self.to(moved(self.co, dim, off), self.core)))
        return out

    def start(self, step):
        for copy in self.copies(step):
            copy.start()

    def wait(self, step):
        for copy in self.copies(step):
            copy.wait()

    def add(self, step):
        if step == 0:

            def add0(i, carry):
                self.a0[i] = (self.part[pl.ds(i * 16, 16), self.core] + self.b0[pl.ds(i * 16, 16)]).reshape(4, 4, 16, 256)
                return carry

            lax.fori_loop(0, 4, add0, 0)
            return
        held = self.a1 if step == 1 else self.a2
        for p, order in enumerate(self.orders):
            came = self.came[step - 1][p]
            at = self.co[order[step - 1]]
            if step == 1:
                own = self.a0[at, :, :, p * 8 : p * 8 + 8] if p == 0 else self.a0[:, at, :, p * 8 : p * 8 + 8]
            else:
                own = self.a1[p, at] if p == 0 else self.a1[p, :, at]
            held[p] = own + came[0] + came[1] + came[2]

    def result(self):
        rows = []
        for p, order in enumerate(self.orders):
            rows.append(self.a2[p, self.co[order[2]]] + self.b3[p, 0] + self.b3[p, 1] + self.b3[p, 2])
        return jnp.concatenate(rows, axis=0)


def sum_scratch():
    W, f32, D = pltpu.VMEM, jnp.float32, pltpu.SemaphoreType.DMA
    return [
        W((64, 16, 256), f32), W((4, 4, 4, 16, 256), f32),
        W((3, 4, 4, 8, 256), f32), W((3, 4, 4, 8, 256), f32), W((2, 4, 4, 8, 256), f32),
        W((3, 4, 8, 256), f32), W((3, 4, 8, 256), f32), W((2, 4, 8, 256), f32),
        W((2, 3, 8, 256), f32), D((4, 2, 3)), D((4, 2, 3)),
    ]


def weight_scratch(size):
    bf = jnp.bfloat16
    return [pltpu.VMEM((256, 2048), bf), pltpu.VMEM((2048, 256), bf), pltpu.VMEM((size, 2048), bf), pltpu.VMEM((size, 256), bf), pltpu.SemaphoreType.DMA((2,))]


def update_rows(u_ref, x_ref, q, size, first, second, hidden_ref, normed_ref):
    def united():
        return u_ref[pl.ds(64 + q * (size // 32), size // 32)].reshape(size, 256)

    u = united()
    normed_ref[...] = (u * lax.rsqrt(jnp.mean(u * u, axis=-1, keepdims=True) + epsilon)).astype(jnp.bfloat16)
    for n in range(0, 2048, 256):
        value = jnp.dot(normed_ref[...], first[:, n : n + 256], preferred_element_type=jnp.float32)
        hidden_ref[:, n : n + 256] = jnp.maximum(value, 0.0).astype(jnp.bfloat16)
    total = united() + jnp.dot(hidden_ref[...], second[...], preferred_element_type=jnp.float32)
    x_ref[pl.ds(q * (size // 128), size // 128)] = total.astype(jnp.bfloat16).reshape(size // 128, 128, 256)


def route_scratch(chunks):
    bf, D = jnp.bfloat16, pltpu.SemaphoreType.DMA
    scratch = [pltpu.VMEM((4, 4, 4, 2, 16, 256), bf)]
    scratch += [pltpu.VMEM((32, n, 256), bf) for lo, n in ROWS for _ in range(3)]
    scratch += [pltpu.VMEM((4, 4, 2, 4, n, 256), bf) for lo, n in ROWS]
    scratch += [pltpu.VMEM((3, 4, 2, 4, n, 256), bf) for lo, n in ROWS]
    scratch += [D((3, 4)), D((3, 4)), D, D((3, chunks, 3)), D((3, chunks, 3)), D((3, 4, 3)), D((3, 4, 3)), D((3, 4, 8)), D((3, 4, 8)), D((12,))]
    return scratch + [D((4, 3)), D((4, 3))]


def exchange(x, send_list, hubs, place):
    bf, f32 = jnp.bfloat16, jnp.float32
    V = pl.BlockSpec(memory_space=pltpu.VMEM)
    return pl.pallas_call(
        functools.partial(exchange_kernel, False, 4),
        out_shape=(
            jax.ShapeDtypeStruct((4, 4, 4, 2, 128, 256), bf),
            jax.ShapeDtypeStruct((2048, 256), bf),
            jax.ShapeDtypeStruct((12, 128), jnp.int32),
        ),
        in_specs=[V, V, V, pl.BlockSpec(memory_space=pltpu.SMEM)],
        out_specs=(pl.BlockSpec(memory_space=pltpu.HBM), V, V),
        scratch_shapes=[pltpu.SMEM((12, 128), jnp.int32), pltpu.VMEM((2048, 256), f32), pltpu.VMEM((2048, 256), f32)] + route_scratch(4),
        compiler_params=pltpu.CompilerParams(collective_id=0, has_side_effects=True, vmem_limit_bytes=60 * 2**20),
        name="exchange",
    )(x, send_list, hubs, place)


def update_exchange(u, near, w_in, w_out):
    bf = jnp.bfloat16
    V, A = pl.BlockSpec(memory_space=pltpu.VMEM), pl.BlockSpec(memory_space=pl.ANY)
    return pl.pallas_call(
        functools.partial(exchange_kernel, True, 8),
        out_shape=(
            jax.ShapeDtypeStruct((4, 4, 4, 2, 128, 256), bf),
            jax.ShapeDtypeStruct((2048, 256), bf),
            jax.ShapeDtypeStruct((32, 128, 256), bf),
        ),
        in_specs=[V, pl.BlockSpec(memory_space=pltpu.SMEM), A, A],
        out_specs=(pl.BlockSpec(memory_space=pltpu.HBM), V, V),
        scratch_shapes=weight_scratch(512) + sum_scratch() + route_scratch(8),
        compiler_params=pltpu.CompilerParams(collective_id=1, has_side_effects=True, vmem_limit_bytes=60 * 2**20),
        name="update_exchange",
    )(u.reshape(192, 2, 16, 256), near, w_in, w_out)


GROUP = 64
BATCH = 16


def tiles_kernel(last, rows_ref, cols_ref, count_ref, place_ref, tiles_ref, x_ref, hubs_ref, in_ref, out_ref, *rest):
    group = pl.program_id(0)
    hub_count, own_count, remote_groups = 16, 32, 128 // GROUP
    table = rest[-1]
    count = count_ref[0]
    position = lax.axis_index("dev")

    def near(block):
        return jnp.where(block < hub_count, block, block - position * own_count)

    @pl.when(group == 0)
    def _():
        def hub(b, carry):
            block = hubs_ref[b]
            out_ref[b] = jnp.where(position == 0, block.astype(jnp.float32), 0.0)
            table[b] = block
            return carry

        lax.fori_loop(0, hub_count, hub, 0)

        def own(b, carry):
            block = x_ref[b]
            out_ref[hub_count + b] = block.astype(jnp.float32)
            table[hub_count + b] = block
            return carry

        lax.fori_loop(0, own_count, own, 0)

    def add(items):
        products = [jnp.dot(tile, block, preferred_element_type=jnp.float32) for slot, tile, block in items]
        for (slot, tile, block), product in zip(items, products):
            row = near(rows_ref[slot])
            out_ref[row] = out_ref[row] + product

    live = jnp.clip(count - group * GROUP, 0, GROUP)

    @pl.when(group < remote_groups)
    def _():
        def step(t, carry):
            add([(group * GROUP + t * BATCH + s, tiles_ref[t * BATCH + s], in_ref[t * BATCH + s]) for s in range(BATCH)])
            return carry

        lax.fori_loop(0, GROUP // BATCH, step, 0)

    @pl.when(group >= remote_groups)
    def _():
        def local(s):
            slot = group * GROUP + s
            return slot, tiles_ref[s], table[near(cols_ref[slot - 128])]

        def step(t, carry):
            add([local(t * BATCH + s) for s in range(BATCH)])
            return carry

        full = live // BATCH
        lax.fori_loop(0, full, step, 0)
        lax.fori_loop(full * BATCH, live, lambda s, carry: (add([local(s)]), carry)[1], 0)

    if last:
        perm_ref = rest[0]

        @pl.when(group == pl.num_programs(0) - 1)
        def _():
            def rows32(g, carry):
                block = out_ref[g // 4, pl.ds(lax.rem(g, 4) * 32, 32), :]
                for r in range(32):
                    perm_ref[pl.ds(place_ref[g * 32 + r], 1), :] = block[r : r + 1]
                return carry

            lax.fori_loop(0, place_ref.shape[0] // 32, rows32, 0)


def sum_tiles(last, rows, cols, count, place, tiles, x, hubs, landed):
    capacity = tiles.shape[0]
    f32 = jnp.float32
    groups = -(-capacity // GROUP)

    def full(*shape):
        return pl.BlockSpec(shape, lambda g, *s: (0,) * len(shape))

    out_shape = [jax.ShapeDtypeStruct((48, 128, 256), f32)]
    out_specs = [full(48, 128, 256)]
    if last:
        out_shape.append(jax.ShapeDtypeStruct((2048, 256), f32))
        out_specs.append(full(2048, 256))
    return pl.pallas_call(
        functools.partial(tiles_kernel, last),
        grid_spec=pltpu.PrefetchScalarGridSpec(
            num_scalar_prefetch=4,
            grid=(groups,),
            in_specs=[
                pl.BlockSpec((GROUP, 128, 128), lambda g, rows, cols, count, place: (jnp.minimum(g, (count[0] - 1) // GROUP), 0, 0)),
                full(32, 128, 256),
                full(16, 128, 256),
                pl.BlockSpec((GROUP, 128, 256), lambda g, *s: (jnp.minimum(g, 128 // GROUP - 1), 0, 0)),
            ],
            out_specs=out_specs,
            scratch_shapes=[pltpu.VMEM((48, 128, 256), jnp.bfloat16)],
        ),
        out_shape=out_shape,
        compiler_params=pltpu.CompilerParams(dimension_semantics=("arbitrary",), vmem_limit_bytes=60 * 2**20),
        name="sum_tiles",
    )(rows, cols, count, place, tiles, x, hubs.reshape(16, 128, 256), landed.reshape(128, 128, 256))


def feed_forward(united, first, second):
    scale = lax.rsqrt(jnp.mean(united * united, axis=-1, keepdims=True) + epsilon)
    normed = (united * scale).astype(jnp.bfloat16)
    total = united
    step = 512
    for n in range(0, first.shape[1], step):
        hidden = jnp.dot(normed, first[:, n : n + step], preferred_element_type=jnp.float32)
        hidden = jnp.maximum(hidden, 0.0).astype(jnp.bfloat16)
        total = total + jnp.dot(hidden, second[n : n + step, :], preferred_element_type=jnp.float32)
    return total.astype(jnp.bfloat16)


def update_kernel(u_ref, part_ref, w1_ref, w2_ref, out_ref, hub_out_ref, first_ref, second_ref, hidden_ref, normed_ref, w_sem, *sum_refs):
    weights = load_weights(w1_ref, w2_ref, first_ref, second_ref, w_sem, 1)
    co, core = coords()

    def to(co2, core2):
        return (device_of(co2, core2),)

    bar = pltpu.get_barrier_semaphore()
    pl.semaphore_signal(bar, inc=1, device_id=to(co, 1 - core), device_id_type=MESH)
    for dim in range(3):
        for off in (1, 2, 3):
            pl.semaphore_signal(bar, inc=1, device_id=to(moved(co, dim, off), core), device_id_type=MESH)
    pl.semaphore_wait(bar, 10)

    def remote(src, dst, ssem, rsem, dev):
        return pltpu.make_async_remote_copy(src_ref=src, dst_ref=dst, send_sem=ssem, recv_sem=rsem, device_id=dev, device_id_type=MESH)

    sums = HubSum(co, core, remote, to, part_ref, *sum_refs)
    sums.start(0)
    weights()
    size = hidden_ref.shape[0]
    for q in range(4096 // size):
        update_rows(u_ref, out_ref, q, size, first_ref, second_ref, hidden_ref, normed_ref)
        if q == 1:
            sums.wait(0)
            sums.add(0)
        if q == 2:
            sums.start(1)
        if q == 5:
            sums.wait(1)
            sums.add(1)
        if q == 6:
            sums.start(2)
    sums.wait(2)
    sums.add(2)
    sums.start(3)
    sums.wait(3)
    hub_out_ref[...] = feed_forward(sums.result(), first_ref, second_ref)


def update(u, part, w_in, w_out):
    bf = jnp.bfloat16
    V, A = pl.BlockSpec(memory_space=pltpu.VMEM), pl.BlockSpec(memory_space=pl.ANY)
    return pl.pallas_call(
        update_kernel,
        out_shape=(jax.ShapeDtypeStruct((32, 128, 256), bf), jax.ShapeDtypeStruct((16, 256), bf)),
        in_specs=[V, V, A, A],
        out_specs=(V, V),
        scratch_shapes=weight_scratch(512) + sum_scratch(),
        compiler_params=pltpu.CompilerParams(collective_id=2, has_side_effects=True, vmem_limit_bytes=60 * 2**20),
        name="update",
    )(u.reshape(192, 2, 16, 256), part.reshape(-1, 2, 16, 256), w_in, w_out)


def body(peripheral, hubs, tiles, tile_rows, local_cols, tile_count, send_list, hub_place, w_in, w_out):
    x = peripheral.reshape(-1, 128, 256)
    landed, table, near = exchange(x, send_list, hubs, hub_place)
    (u,) = sum_tiles(False, tile_rows, local_cols, tile_count, hub_place, tiles, x, table, landed)
    landed, table, x = update_exchange(u, near, w_in, w_out)
    u, part = sum_tiles(True, tile_rows, local_cols, tile_count, hub_place, tiles, x, table, landed)
    new, hub_new = update(u, part, w_in, w_out)
    return new.reshape(peripheral.shape), hub_new


def solution(mesh):
    split = P("dev")
    in_specs = (split, split, split, split, split, split, split, P(), P(), P())
    return jax.shard_map(body, mesh=mesh, in_specs=in_specs, out_specs=(split, split), check_vma=False)
```

```python
import functools
import jax
import jax.numpy as jnp
from jax import lax
from jax.sharding import PartitionSpec as P
from jax.experimental import pallas as pl
from jax.experimental.pallas import tpu as pltpu

MESH = pl.DeviceIdType.MESH
PARTS = ((0, 88, 0, 128), (0, 88, 128, 128), (88, 40, 0, 256))
epsilon = 1e-06


def coords():
    me = lax.axis_index("dev")
    return [me // 32, lax.rem(me // 8, 4), lax.rem(me // 2, 4)], lax.rem(me, 2)


def device_of(co, core):
    return ((co[0] * 4 + co[1]) * 4 + co[2]) * 2 + core


def moved(co, dim, off):
    out = list(co)
    out[dim] = lax.rem(co[dim] + off, 4)
    return out


def exchange_kernel(fused, CH, *refs):
    if fused:
        far_ref, lists, w1_ref, w2_ref, in_ref, hubs_ref, x_ref = refs[:7]
        u_ref, u_sem, first_ref, second_ref, hidden_ref, normed_ref, w_sem = refs[7:14]
        sum_refs = refs[14:25]
        refs = refs[25:]
    else:
        x_ref, list_ref, hub_ref, place_ref, in_ref, hubs_ref, near_ref, lists, wide, ordered = refs[:10]
        refs = refs[10:]
    exchange_steps(fused, CH, locals(), *refs)


def exchange_steps(fused, CH, given, gathered, t00, t01, t02, t10, t11, t12, t20, t21, t22, s0, s1, s2, r0, r1, r2,
                    list_sem, list_send, smem_sem, ag_send, ag_recv, p2_send, p2_recv, p3_send, p3_recv, local_sem, hub_send, hub_recv):
    x_ref, in_ref, hubs_ref, lists = given["x_ref"], given["in_ref"], given["hubs_ref"], given["lists"]
    if fused:
        sums_in = load_sums(given["far_ref"], given["far_ref"], given["u_ref"], given["u_sem"])
        weights = load_weights(given["w1_ref"], given["w2_ref"], given["first_ref"], given["second_ref"], given["w_sem"], 0)
    else:
        list_ref, hub_ref, place_ref, near_ref = given["list_ref"], given["hub_ref"], given["place_ref"], given["near_ref"]
    tabs = ((t00, t01, t02), (t10, t11, t12), (t20, t21, t22))
    stage, relay = (s0, s1, s2), (r0, r1, r2)
    co, core = coords()
    blocks = x_ref.shape[0]
    per = blocks // CH

    def to(co2, core2):
        return (device_of(co2, core2),)

    bar = pltpu.get_barrier_semaphore()
    for dim in range(3):
        for off in (1, 2, 3):
            for flip in (0, 1):
                pl.semaphore_signal(bar, inc=1, device_id=to(moved(co, dim, off), lax.rem(core + flip, 2)), device_id_type=MESH)
    pl.semaphore_signal(bar, inc=1, device_id=to(co, 1 - core), device_id_type=MESH)
    pl.semaphore_wait(bar, 19)

    def remote(src, dst, ssem, rsem, dev):
        return pltpu.make_async_remote_copy(src_ref=src, dst_ref=dst, send_sem=ssem, recv_sem=rsem, device_id=dev, device_id_type=MESH)

    def list_copy(dim, off):
        return remote(list_ref, near_ref.at[pl.ds(dim * 4 + 4 - off, 1)], list_send.at[dim, off], list_sem.at[dim, 4 - off], to(moved(co, dim, off), core))

    def hub_copy(step, off):
        if step == 3:
            part = gathered.at[:, :, :, core]
            return remote(part, part, hub_send.at[3, 0], hub_recv.at[3, 0], to(co, 1 - core))
        dim = 2 - step
        part = (gathered.at[co[0], co[1], co[2], core], gathered.at[co[0], co[1], :, core], gathered.at[co[0], :, :, core])[step]
        return remote(part, part, hub_send.at[step, off - 1], hub_recv.at[step, 3 - off], to(moved(co, dim, off), core))

    def hub_start(step):
        for off in (1, 2, 3) if step < 3 else (1,):
            hub_copy(step, off).start()

    def hub_wait(step):
        for off in (1, 2, 3) if step < 3 else (1,):
            hub_copy(step, off).wait()

    def ag_copy(p, q, direction):
        lo, n, left, lanes = PARTS[p]
        off = 1 if direction == 0 else 3
        seen = 4 - off
        return remote(x_ref.at[pl.ds(q * per, per), pl.ds(lo, n), pl.ds(left, lanes)], tabs[p][seen - 1].at[pl.ds(q * per, per)],
                      ag_send.at[p, q, direction], ag_recv.at[p, q, seen - 1], to(moved(co, p, off), core))

    def relay_copy(p, q):
        off = 1 if q % 2 == 0 else 3
        seen = 4 - off
        return remote(tabs[p][seen - 1].at[pl.ds(q * per, per)], tabs[p][1].at[pl.ds(q * per, per)],
                      ag_send.at[p, q, 2], ag_recv.at[p, q, 1], to(moved(co, p, off), core))

    def ag_start(q):
        for p in range(3):
            for direction in (0, 1) if q % 2 == 0 else (1, 0):
                ag_copy(p, q, direction).start()

    def relay_on(q):
        for p in range(3):
            ag_wait(ag_recv, tabs, p, q, 2 if q % 2 == 0 else 0, per)
            relay_copy(p, q).start()

    def assemble(p, i, js):
        lo, n, left, lanes = PARTS[p]
        d1, d2 = (p + 1) % 3, (p + 2) % 3
        where = lax.rem(co[p] + i, 4)
        row = 0 if i == 0 else p * 4 + i
        for j in js:
            def piece(m, carry, j=j):
                k, flip = m // 2, lax.rem(m, 2)
                target = device_of(moved(moved(co, d1, j), d2, k), flip)
                b = lists[row, target]
                value = x_ref[b, lo:lo + n, left:left + lanes] if i == 0 else tabs[p][i - 1][b]
                stage[p][j, k, flip, where] = value
                return carry
            lax.fori_loop(0, 8, piece, 0)

    def p2_copy(p, i, j):
        d1 = (p + 1) % 3
        where = lax.rem(co[p] + i, 4)
        return remote(stage[p].at[j, :, :, where], relay[p].at[3 - j, :, :, where],
                      p2_send.at[p, i, j - 1], p2_recv.at[p, i, 3 - j], to(moved(co, d1, j), core))

    def send2(p, i):
        for j in (1, 3, 2):
            p2_copy(p, i, j).start()

    def pick(p, i):
        for q in range(CH):
            if i == 2 or (i == 1 and q % 2 == 0) or (i == 3 and q % 2 == 1):
                ag_wait(ag_recv, tabs, p, q, i - 1, per)
        assemble(p, i, (1, 3, 2, 0))

    def pass_on(i):
        for p in range(3):
            pick(p, i)
            if p:
                send2(p - 1, i)
        send2(2, i)

    place = ((0, 1, 2), (2, 0, 1), (1, 2, 0))

    def landing(p, s1, s2, s_core):
        lo, n, left, lanes = PARTS[p]
        idx = [None, None, None]
        idx[p] = slice(None)
        idx[(p + 1) % 3] = s1
        idx[(p + 2) % 3] = s2
        return in_ref.at[idx[0], idx[1], idx[2], s_core, pl.ds(lo, n), pl.ds(left, lanes)]

    def p3_copy(p, j, k, flip):
        d1, d2 = (p + 1) % 3, (p + 2) % 3
        src = stage[p].at[0, k, lax.rem(core + flip, 2)] if j == 0 else relay[p].at[j - 1, k, lax.rem(core + flip, 2)]
        s1 = lax.rem(co[d1] + j, 4)
        dst = landing(p, s1, co[d2], core)
        if k == 0 and flip == 0:
            return pltpu.make_async_copy(src, dst, local_sem.at[p * 4 + j])
        return remote(src, dst, p3_send.at[p, j, k * 2 + flip], p3_recv.at[p, j, k * 2 + flip], to(moved(co, d2, k), lax.rem(core + flip, 2)))

    def send3(p, j):
        for k in (1, 3, 2, 0):
            for flip in (0, 1):
                p3_copy(p, j, k, flip).start()

    def finish(j):
        for p in range(3):
            for i in range(4):
                p2_wait(p2_recv, relay, p, i, j - 1)
            send3(p, j)

    def own_pass():
        for p in range(3):
            assemble(p, 0, (1, 3, 2, 0))
            if p:
                send2(p - 1, 0)
        send2(2, 0)

    if fused:
        sums = HubSum(co, core, remote, to, given["u_ref"], *given["sum_refs"])
        sums_in(STEPS)
        sums.start(0)
        weights()
        first_ref, second_ref = given["first_ref"], given["second_ref"]
        size = 4096 // CH
        for q in range(CH):
            sums_in(q)
            update_rows(given["u_ref"], x_ref, q, size, first_ref, second_ref, given["hidden_ref"], given["normed_ref"])
            if q == 2:
                sums.start(1)
            if q == 6:
                sums.start(2)
            if q >= 1:
                ag_start(q - 1)
            if q == 1:
                sums.wait(0)
                sums.add(0)
            if q == 5:
                sums.wait(1)
                sums.add(1)
            if q >= 4:
                relay_on(q - 4)
        assemble(0, 0, (1, 3, 2, 0))
        ag_start(CH - 1)
        relay_on(CH - 4)
        assemble(1, 0, (1, 3, 2, 0))
        sums.wait(2)
        sums.add(2)
        relay_on(CH - 3)
        assemble(2, 0, (1, 3, 2, 0))
        sums.start(3)
        relay_on(CH - 2)
        for p in range(3):
            send2(p, 0)
        relay_on(CH - 1)
        pick(0, 1)
        pick(1, 1)
        pick(2, 1)
        sums.wait(3)
        gathered[co[0], co[1], co[2], core] = feed_forward(sums.result(), first_ref, second_ref)
        pick(0, 3)
        hub_start(0)
        for p in range(3):
            send2(p, 1)
        pick(1, 3)
        send2(0, 3)
        pick(2, 3)
        send2(1, 3)
        send2(2, 3)
        pass_on(2)
        hub_wait(0)
        hub_start(1)
        for p in range(3):
            send3(p, 0)
        finish(1)
        finish(3)
        hub_wait(1)
        hub_start(2)
        finish(2)
        hub_wait(2)
        hub_start(3)
    else:
        for dim in range(3):
            for off in (1, 2, 3):
                list_copy(dim, off).start()
        hub_own = pltpu.make_async_copy(hub_ref, gathered.at[co[0], co[1], co[2], core], local_sem.at[1])
        hub_own.start()
        hub_own.wait()
        hub_start(0)
        for q in range(CH):
            ag_start(q)
        own = pltpu.make_async_copy(list_ref, near_ref.at[pl.ds(0, 1)], local_sem.at[0])
        own.start()
        own.wait()
        for dim in range(3):
            for off in (1, 2, 3):
                list_copy(dim, off).wait_recv()
        fetch = pltpu.make_async_copy(near_ref, lists, smem_sem)
        fetch.start()
        fetch.wait()
        own_pass()
        hub_wait(0)
        hub_start(1)
        for q in range(CH):
            relay_on(q)
        hub_wait(1)
        hub_start(2)
        pass_on(1)
        pass_on(3)
        hub_wait(2)
        hub_start(3)
        pass_on(2)
        for p in range(3):
            send3(p, 0)
        for j in (1, 3, 2):
            finish(j)
    hub_wait(3)
    if not fused:
        wide, ordered = given["wide"], given["ordered"]
        wide[...] = gathered[...].astype(jnp.float32).reshape(wide.shape)

        def rows8(g, carry):
            for r in range(8):
                ordered[pl.ds(g * 8 + r, 1), :] = wide[pl.ds(place_ref[g * 8 + r], 1), :]
            return carry

        lax.fori_loop(0, wide.shape[0] // 8, rows8, 0)
        hubs_ref[...] = ordered[...].astype(jnp.bfloat16)
    else:
        hubs_ref[...] = gathered[...].reshape(hubs_ref.shape)
    for p in range(3):
        for j in range(4):
            for k in range(4):
                for flip in (0, 1):
                    if k == 0 and flip == 0:
                        p3_copy(p, j, k, flip).wait()
                    else:
                        p3_copy(p, j, k, flip).wait()
    for p in range(3):
        for q in range(CH):
            ag_copy(p, q, 0).wait_send()
            ag_copy(p, q, 1).wait_send()
            relay_copy(p, q).wait_send()
        for i in range(4):
            for j in (1, 2, 3):
                p2_copy(p, i, j).wait_send()
    if not fused:
        for dim in range(3):
            for off in (1, 2, 3):
                list_copy(dim, off).wait_send()


def ag_wait(sem, tabs, p, q, slot, per):
    ref = tabs[p][slot].at[pl.ds(q * per, per)]
    pltpu.make_async_copy(ref, ref, sem.at[p, q, slot]).wait()


def p2_wait(sem, relay, p, i, slot):
    ref = relay[p].at[slot, :, :, 0]
    pltpu.make_async_copy(ref, ref, sem.at[p, i, slot]).wait()


STEPS = 8


def load_sums(far_ref, part_ref, u_ref, sem):
    rows = 128 // STEPS
    copies = [pltpu.make_async_copy(far_ref.at[pl.ds(64 + q * rows, rows)], u_ref.at[pl.ds(64 + q * rows, rows)], sem.at[q]) for q in range(STEPS)]
    copies.append(pltpu.make_async_copy(part_ref.at[pl.ds(0, 64)], u_ref.at[pl.ds(0, 64)], sem.at[STEPS]))
    copies[0].start()
    copies[STEPS].start()
    for q in range(1, STEPS):
        copies[q].start()
    return lambda q: copies[q].wait()


def load_weights(w1_ref, w2_ref, first_ref, second_ref, sem, layer):
    copies = [
        pltpu.make_async_copy(w1_ref.at[layer], first_ref, sem.at[0]),
        pltpu.make_async_copy(w2_ref.at[layer], second_ref, sem.at[1]),
    ]
    for copy in copies:
        copy.start()

    def wait():
        for copy in copies:
            copy.wait()

    return wait


class HubSum:
    orders = ((0, 1, 2), (1, 2, 0))

    def __init__(self, co, core, remote, to, part, b0, a0, b1a, b1b, a1, b2a, b2b, a2, b3, send, recv):
        self.co, self.core, self.remote, self.to, self.part = co, core, remote, to, part
        self.b0, self.a0, self.a1, self.a2 = b0, a0, a1, a2
        self.came = ((b1a, b1b), (b2a, b2b), (b3.at[0], b3.at[1]))
        self.b3, self.send, self.recv = b3, send, recv

    def source(self, step, p, at):
        if step == 1:
            rows = pl.ds(p * 8, 8)
            return self.a0.at[at, :, :, rows] if p == 0 else self.a0.at[:, at, :, rows]
        if step == 2:
            return self.a1.at[p, at] if p == 0 else self.a1.at[p, :, at]
        return self.a2.at[p, at]

    def copies(self, step):
        if step == 0:
            return [self.remote(self.part.at[0:64, 1 - self.core], self.b0, self.send.at[0, 0, 0], self.recv.at[0, 0, 0], self.to(self.co, 1 - self.core))]
        out = []
        for p, order in enumerate(self.orders):
            dim = order[step - 1]
            for off in (1, 2, 3):
                src = self.source(step, p, lax.rem(self.co[dim] + off, 4))
                out.append(self.remote(src, self.came[step - 1][p].at[3 - off], self.send.at[step, p, off - 1], self.recv.at[step, p, 3 - off], self.to(moved(self.co, dim, off), self.core)))
        return out

    def start(self, step):
        for copy in self.copies(step):
            copy.start()

    def wait(self, step):
        for copy in self.copies(step):
            copy.wait()

    def add(self, step):
        if step == 0:

            def add0(i, carry):
                self.a0[i] = (self.part[pl.ds(i * 16, 16), self.core] + self.b0[pl.ds(i * 16, 16)]).reshape(4, 4, 16, 256)
                return carry

            lax.fori_loop(0, 4, add0, 0)
            return
        held = self.a1 if step == 1 else self.a2
        for p, order in enumerate(self.orders):
            came = self.came[step - 1][p]
            at = self.co[order[step - 1]]
            if step == 1:
                own = self.a0[at, :, :, p * 8 : p * 8 + 8] if p == 0 else self.a0[:, at, :, p * 8 : p * 8 + 8]
            else:
                own = self.a1[p, at] if p == 0 else self.a1[p, :, at]
            held[p] = own + came[0] + came[1] + came[2]

    def result(self):
        rows = []
        for p, order in enumerate(self.orders):
            rows.append(self.a2[p, self.co[order[2]]] + self.b3[p, 0] + self.b3[p, 1] + self.b3[p, 2])
        return jnp.concatenate(rows, axis=0)


def sum_scratch():
    W, f32, D = pltpu.VMEM, jnp.float32, pltpu.SemaphoreType.DMA
    return [
        W((64, 16, 256), f32), W((4, 4, 4, 16, 256), f32),
        W((3, 4, 4, 8, 256), f32), W((3, 4, 4, 8, 256), f32), W((2, 4, 4, 8, 256), f32),
        W((3, 4, 8, 256), f32), W((3, 4, 8, 256), f32), W((2, 4, 8, 256), f32),
        W((2, 3, 8, 256), f32), D((4, 2, 3)), D((4, 2, 3)),
    ]


def weight_scratch(size):
    bf = jnp.bfloat16
    return [pltpu.VMEM((192, 2, 16, 256), jnp.float32), pltpu.SemaphoreType.DMA((STEPS + 1,)), pltpu.VMEM((256, 2048), bf), pltpu.VMEM((2048, 256), bf), pltpu.VMEM((size, 2048), bf), pltpu.VMEM((size, 256), bf), pltpu.SemaphoreType.DMA((2,))]


def update_rows(u_ref, x_ref, q, size, first, second, hidden_ref, normed_ref):
    def united():
        return u_ref[pl.ds(64 + q * (size // 32), size // 32)].reshape(size, 256)

    u = united()
    normed_ref[...] = (u * lax.rsqrt(jnp.mean(u * u, axis=-1, keepdims=True) + epsilon)).astype(jnp.bfloat16)
    for n in range(0, 2048, 256):
        value = jnp.dot(normed_ref[...], first[:, n : n + 256], preferred_element_type=jnp.float32)
        hidden_ref[:, n : n + 256] = jnp.maximum(value, 0.0).astype(jnp.bfloat16)
    total = united() + jnp.dot(hidden_ref[...], second[...], preferred_element_type=jnp.float32)
    x_ref[pl.ds(q * (size // 128), size // 128)] = total.astype(jnp.bfloat16).reshape(size // 128, 128, 256)


def route_scratch(chunks):
    bf, D = jnp.bfloat16, pltpu.SemaphoreType.DMA
    scratch = [pltpu.VMEM((4, 4, 4, 2, 16, 256), bf)]
    scratch += [pltpu.VMEM((32, n, w), bf) for lo, n, left, w in PARTS for _ in range(3)]
    scratch += [pltpu.VMEM((4, 4, 2, 4, n, w), bf) for lo, n, left, w in PARTS]
    scratch += [pltpu.VMEM((3, 4, 2, 4, n, w), bf) for lo, n, left, w in PARTS]
    scratch += [D((3, 4)), D((3, 4)), D, D((3, chunks, 3)), D((3, chunks, 3)), D((3, 4, 3)), D((3, 4, 3)), D((3, 4, 8)), D((3, 4, 8)), D((12,))]
    return scratch + [D((4, 3)), D((4, 3))]


def exchange(x, send_list, hubs, place):
    bf, f32 = jnp.bfloat16, jnp.float32
    V = pl.BlockSpec(memory_space=pltpu.VMEM)
    return pl.pallas_call(
        functools.partial(exchange_kernel, False, 4),
        out_shape=(
            jax.ShapeDtypeStruct((4, 4, 4, 2, 128, 256), bf),
            jax.ShapeDtypeStruct((2048, 256), bf),
            jax.ShapeDtypeStruct((12, 128), jnp.int32),
        ),
        in_specs=[V, V, V, pl.BlockSpec(memory_space=pltpu.SMEM)],
        out_specs=(pl.BlockSpec(memory_space=pltpu.HBM), V, V),
        scratch_shapes=[pltpu.SMEM((12, 128), jnp.int32), pltpu.VMEM((2048, 256), f32), pltpu.VMEM((2048, 256), f32)] + route_scratch(4),
        compiler_params=pltpu.CompilerParams(collective_id=0, has_side_effects=True, vmem_limit_bytes=60 * 2**20),
        name="exchange",
    )(x, send_list, hubs, place)


def update_exchange(u, near, w_in, w_out):
    bf = jnp.bfloat16
    V, A = pl.BlockSpec(memory_space=pltpu.VMEM), pl.BlockSpec(memory_space=pl.ANY)
    return pl.pallas_call(
        functools.partial(exchange_kernel, True, 8),
        out_shape=(
            jax.ShapeDtypeStruct((4, 4, 4, 2, 128, 256), bf),
            jax.ShapeDtypeStruct((2048, 256), bf),
            jax.ShapeDtypeStruct((32, 128, 256), bf),
        ),
        in_specs=[A, pl.BlockSpec(memory_space=pltpu.SMEM), A, A],
        out_specs=(pl.BlockSpec(memory_space=pltpu.HBM), V, V),
        scratch_shapes=weight_scratch(512) + sum_scratch() + route_scratch(8),
        compiler_params=pltpu.CompilerParams(collective_id=1, has_side_effects=True, vmem_limit_bytes=60 * 2**20),
        name="update_exchange",
    )(u.reshape(192, 2, 16, 256), near, w_in, w_out)


GROUP = 64
BATCH = 16


def tiles_kernel(last, rows_ref, cols_ref, count_ref, place_ref, tiles_ref, x_ref, hubs_ref, in_ref, out_ref, *rest):
    group = pl.program_id(0)
    hub_count, own_count, remote_groups = 16, 32, 128 // GROUP
    table = rest[-1]
    count = count_ref[0]
    position = lax.axis_index("dev")

    def near(block):
        return jnp.where(block < hub_count, block, block - position * own_count)

    @pl.when(group == 0)
    def _():
        def hub(b, carry):
            block = hubs_ref[b]
            out_ref[b] = jnp.where(position == 0, block.astype(jnp.float32), 0.0)
            table[b] = block
            return carry

        lax.fori_loop(0, hub_count, hub, 0)

        def own(b, carry):
            block = x_ref[b]
            out_ref[hub_count + b] = block.astype(jnp.float32)
            table[hub_count + b] = block
            return carry

        lax.fori_loop(0, own_count, own, 0)

    def add(items):
        products = [jnp.dot(tile, block, preferred_element_type=jnp.float32) for slot, tile, block in items]
        for (slot, tile, block), product in zip(items, products):
            row = near(rows_ref[slot])
            out_ref[row] = out_ref[row] + product

    live = jnp.clip(count - group * GROUP, 0, GROUP)

    @pl.when(group < remote_groups)
    def _():
        def step(t, carry):
            add([(group * GROUP + t * BATCH + s, tiles_ref[t * BATCH + s], in_ref[t * BATCH + s]) for s in range(BATCH)])
            return carry

        lax.fori_loop(0, GROUP // BATCH, step, 0)

    @pl.when(group >= remote_groups)
    def _():
        def local(s):
            slot = group * GROUP + s
            return slot, tiles_ref[s], table[near(cols_ref[slot - 128])]

        def step(t, carry):
            add([local(t * BATCH + s) for s in range(BATCH)])
            return carry

        full = live // BATCH
        lax.fori_loop(0, full, step, 0)
        lax.fori_loop(full * BATCH, live, lambda s, carry: (add([local(s)]), carry)[1], 0)

    if last:
        perm_ref = rest[0]

        @pl.when(group == pl.num_programs(0) - 1)
        def _():
            def rows32(g, carry):
                block = out_ref[g // 4, pl.ds(lax.rem(g, 4) * 32, 32), :]
                for r in range(32):
                    perm_ref[pl.ds(place_ref[g * 32 + r], 1), :] = block[r : r + 1]
                return carry

            lax.fori_loop(0, place_ref.shape[0] // 32, rows32, 0)


def sum_tiles(last, rows, cols, count, place, tiles, x, hubs, landed):
    capacity = tiles.shape[0]
    f32 = jnp.float32
    groups = -(-capacity // GROUP)

    def full(*shape):
        return pl.BlockSpec(shape, lambda g, *s: (0,) * len(shape))

    out_shape = [jax.ShapeDtypeStruct((48, 128, 256), f32)]
    out_specs = [full(48, 128, 256)]
    if last:
        out_shape.append(jax.ShapeDtypeStruct((2048, 256), f32))
        out_specs.append(full(2048, 256))
    return pl.pallas_call(
        functools.partial(tiles_kernel, last),
        grid_spec=pltpu.PrefetchScalarGridSpec(
            num_scalar_prefetch=4,
            grid=(groups,),
            in_specs=[
                pl.BlockSpec((GROUP, 128, 128), lambda g, rows, cols, count, place: (jnp.minimum(g, (count[0] - 1) // GROUP), 0, 0)),
                full(32, 128, 256),
                full(16, 128, 256),
                pl.BlockSpec((GROUP, 128, 256), lambda g, *s: (jnp.minimum(g, 128 // GROUP - 1), 0, 0)),
            ],
            out_specs=out_specs,
            scratch_shapes=[pltpu.VMEM((48, 128, 256), jnp.bfloat16)],
        ),
        out_shape=out_shape,
        compiler_params=pltpu.CompilerParams(dimension_semantics=("arbitrary",), vmem_limit_bytes=60 * 2**20),
        name="sum_tiles",
    )(rows, cols, count, place, tiles, x, hubs.reshape(16, 128, 256), landed.reshape(128, 128, 256))


def feed_forward(united, first, second):
    scale = lax.rsqrt(jnp.mean(united * united, axis=-1, keepdims=True) + epsilon)
    normed = (united * scale).astype(jnp.bfloat16)
    total = united
    step = 512
    for n in range(0, first.shape[1], step):
        hidden = jnp.dot(normed, first[:, n : n + step], preferred_element_type=jnp.float32)
        hidden = jnp.maximum(hidden, 0.0).astype(jnp.bfloat16)
        total = total + jnp.dot(hidden, second[n : n + step, :], preferred_element_type=jnp.float32)
    return total.astype(jnp.bfloat16)


def update_kernel(far_ref, part_ref, w1_ref, w2_ref, out_ref, hub_out_ref, u_ref, u_sem, first_ref, second_ref, hidden_ref, normed_ref, w_sem, *sum_refs):
    sums_in = load_sums(far_ref, part_ref, u_ref, u_sem)
    weights = load_weights(w1_ref, w2_ref, first_ref, second_ref, w_sem, 1)
    co, core = coords()

    def to(co2, core2):
        return (device_of(co2, core2),)

    bar = pltpu.get_barrier_semaphore()
    pl.semaphore_signal(bar, inc=1, device_id=to(co, 1 - core), device_id_type=MESH)
    for dim in range(3):
        for off in (1, 2, 3):
            pl.semaphore_signal(bar, inc=1, device_id=to(moved(co, dim, off), core), device_id_type=MESH)
    pl.semaphore_wait(bar, 10)

    def remote(src, dst, ssem, rsem, dev):
        return pltpu.make_async_remote_copy(src_ref=src, dst_ref=dst, send_sem=ssem, recv_sem=rsem, device_id=dev, device_id_type=MESH)

    sums = HubSum(co, core, remote, to, u_ref, *sum_refs)
    sums_in(STEPS)
    sums.start(0)
    weights()
    size = hidden_ref.shape[0]
    for q in range(STEPS):
        sums_in(q)
        update_rows(u_ref, out_ref, q, size, first_ref, second_ref, hidden_ref, normed_ref)
        if q == 0:
            sums.wait(0)
            sums.add(0)
        if q == 1:
            sums.start(1)
        if q == 5:
            sums.wait(1)
            sums.add(1)
        if q == 6:
            sums.start(2)
    sums.wait(2)
    sums.add(2)
    sums.start(3)
    sums.wait(3)
    hub_out_ref[...] = feed_forward(sums.result(), first_ref, second_ref)


def update(u, part, w_in, w_out):
    bf = jnp.bfloat16
    V, A = pl.BlockSpec(memory_space=pltpu.VMEM), pl.BlockSpec(memory_space=pl.ANY)
    return pl.pallas_call(
        update_kernel,
        out_shape=(jax.ShapeDtypeStruct((32, 128, 256), bf), jax.ShapeDtypeStruct((16, 256), bf)),
        in_specs=[A, A, A, A],
        out_specs=(V, V),
        scratch_shapes=weight_scratch(512) + sum_scratch(),
        compiler_params=pltpu.CompilerParams(collective_id=2, has_side_effects=True, vmem_limit_bytes=60 * 2**20),
        name="update",
    )(u.reshape(192, 2, 16, 256), part.reshape(-1, 2, 16, 256), w_in, w_out)


def body(peripheral, hubs, tiles, tile_rows, local_cols, tile_count, send_list, hub_place, w_in, w_out):
    x = peripheral.reshape(-1, 128, 256)
    landed, table, near = exchange(x, send_list, hubs, hub_place)
    (u,) = sum_tiles(False, tile_rows, local_cols, tile_count, hub_place, tiles, x, table, landed)
    landed, table, x = update_exchange(u, near, w_in, w_out)
    u, part = sum_tiles(True, tile_rows, local_cols, tile_count, hub_place, tiles, x, table, landed)
    new, hub_new = update(u, part, w_in, w_out)
    return new.reshape(peripheral.shape), hub_new


def solution(mesh):
    split = P("dev")
    in_specs = (split, split, split, split, split, split, split, P(), P(), P())
    return jax.shard_map(body, mesh=mesh, in_specs=in_specs, out_specs=(split, split), check_vma=False)
```

```python
import functools
import jax
import jax.numpy as jnp
from jax import lax
from jax.sharding import PartitionSpec as P
from jax.experimental import pallas as pl
from jax.experimental.pallas import tpu as pltpu

MESH = pl.DeviceIdType.MESH
PARTS = ((0, 88, 0, 128), (0, 88, 128, 128), (88, 40, 0, 256))
epsilon = 1e-06


def coords():
    me = lax.axis_index("dev")
    return [me // 32, lax.rem(me // 8, 4), lax.rem(me // 2, 4)], lax.rem(me, 2)


def device_of(co, core):
    return ((co[0] * 4 + co[1]) * 4 + co[2]) * 2 + core


def moved(co, dim, off):
    out = list(co)
    out[dim] = lax.rem(co[dim] + off, 4)
    return out


def exchange_kernel(fused, CH, *refs):
    if fused:
        far_ref, lists, w1_ref, w2_ref, in_ref, hubs_ref, x_ref = refs[:7]
        u_ref, u_sem, first_ref, second_ref, hidden_ref, normed_ref, w_sem = refs[7:14]
        sum_refs = refs[14:25]
        refs = refs[25:]
    else:
        x_ref, list_ref, hub_ref, place_ref, in_ref, hubs_ref, near_ref, lists, wide, ordered = refs[:10]
        refs = refs[10:]
    exchange_steps(fused, CH, locals(), *refs)


def exchange_steps(fused, CH, given, gathered, t00, t01, t02, t10, t11, t12, t20, t21, t22, s0, s1, s2, r0, r1, r2,
                    list_sem, list_send, smem_sem, ag_send, ag_recv, p2_send, p2_recv, p3_send, p3_recv, local_sem, hub_send, hub_recv):
    x_ref, in_ref, hubs_ref, lists = given["x_ref"], given["in_ref"], given["hubs_ref"], given["lists"]
    if fused:
        sums_in = load_sums(given["far_ref"], given["far_ref"], given["u_ref"], given["u_sem"])
        weights = load_weights(given["w1_ref"], given["w2_ref"], given["first_ref"], given["second_ref"], given["w_sem"], 0)
    else:
        list_ref, hub_ref, place_ref, near_ref = given["list_ref"], given["hub_ref"], given["place_ref"], given["near_ref"]
    tabs = ((t00, t01, t02), (t10, t11, t12), (t20, t21, t22))
    stage, relay = (s0, s1, s2), (r0, r1, r2)
    co, core = coords()
    blocks = x_ref.shape[0]
    per = blocks // CH

    def to(co2, core2):
        return (device_of(co2, core2),)

    bar = pltpu.get_barrier_semaphore()
    for dim in range(3):
        for off in (1, 2, 3):
            for flip in (0, 1):
                pl.semaphore_signal(bar, inc=1, device_id=to(moved(co, dim, off), lax.rem(core + flip, 2)), device_id_type=MESH)
    pl.semaphore_signal(bar, inc=1, device_id=to(co, 1 - core), device_id_type=MESH)
    pl.semaphore_wait(bar, 19)

    def remote(src, dst, ssem, rsem, dev):
        return pltpu.make_async_remote_copy(src_ref=src, dst_ref=dst, send_sem=ssem, recv_sem=rsem, device_id=dev, device_id_type=MESH)

    def list_copy(dim, off):
        return remote(list_ref, near_ref.at[pl.ds(dim * 4 + 4 - off, 1)], list_send.at[dim, off], list_sem.at[dim, 4 - off], to(moved(co, dim, off), core))

    def hub_copy(step, off):
        if step == 3:
            part = gathered.at[:, :, :, core]
            return remote(part, part, hub_send.at[3, 0], hub_recv.at[3, 0], to(co, 1 - core))
        half, off = off // 4, off % 4
        rows = pl.ds(half * 8, 8)
        dim = ((2, 1, 0), (0, 2, 1))[half][step]
        x, y, z = co
        every = slice(None)
        at = (((x, y, z), (x, y, every), (x, every, every)), ((x, y, z), (every, y, z), (every, y, every)))[half][step]
        part = gathered.at[at[0], at[1], at[2], core, rows]
        return remote(part, part, hub_send.at[step, half * 3 + off - 1], hub_recv.at[step, half * 3 + 3 - off], to(moved(co, dim, off), core))

    def hub_start(step):
        for off in (1, 2, 3, 5, 6, 7) if step < 3 else (1,):
            hub_copy(step, off).start()

    def hub_wait(step):
        for off in (1, 2, 3, 5, 6, 7) if step < 3 else (1,):
            hub_copy(step, off).wait()

    def ag_copy(p, q, direction):
        lo, n, left, lanes = PARTS[p]
        off = 1 if direction == 0 else 3
        seen = 4 - off
        return remote(x_ref.at[pl.ds(q * per, per), pl.ds(lo, n), pl.ds(left, lanes)], tabs[p][seen - 1].at[pl.ds(q * per, per)],
                      ag_send.at[p, q, direction], ag_recv.at[p, q, seen - 1], to(moved(co, p, off), core))

    def relay_copy(p, q):
        off = 1 if q % 2 == 0 else 3
        seen = 4 - off
        return remote(tabs[p][seen - 1].at[pl.ds(q * per, per)], tabs[p][1].at[pl.ds(q * per, per)],
                      ag_send.at[p, q, 2], ag_recv.at[p, q, 1], to(moved(co, p, off), core))

    def ag_start(q):
        for p in range(3):
            for direction in (0, 1) if q % 2 == 0 else (1, 0):
                ag_copy(p, q, direction).start()

    def relay_on(q):
        for p in range(3):
            ag_wait(ag_recv, tabs, p, q, 2 if q % 2 == 0 else 0, per)
            relay_copy(p, q).start()

    def assemble(p, i, js):
        lo, n, left, lanes = PARTS[p]
        d1, d2 = (p + 1) % 3, (p + 2) % 3
        where = lax.rem(co[p] + i, 4)
        row = 0 if i == 0 else p * 4 + i
        for j in js:
            def piece(m, carry, j=j):
                k, flip = m // 2, lax.rem(m, 2)
                target = device_of(moved(moved(co, d1, j), d2, k), flip)
                b = lists[row, target]
                value = x_ref[b, lo:lo + n, left:left + lanes] if i == 0 else tabs[p][i - 1][b]
                stage[p][j, k, flip, where] = value
                return carry
            lax.fori_loop(0, 8, piece, 0)

    def p2_copy(p, i, j):
        d1 = (p + 1) % 3
        where = lax.rem(co[p] + i, 4)
        return remote(stage[p].at[j, :, :, where], relay[p].at[3 - j, :, :, where],
                      p2_send.at[p, i, j - 1], p2_recv.at[p, i, 3 - j], to(moved(co, d1, j), core))

    def send2(p, i):
        for j in (1, 3, 2):
            p2_copy(p, i, j).start()

    def pick(p, i):
        for q in range(CH):
            if i == 2 or (i == 1 and q % 2 == 0) or (i == 3 and q % 2 == 1):
                ag_wait(ag_recv, tabs, p, q, i - 1, per)
        assemble(p, i, (1, 3, 2, 0))

    def pass_on(i):
        for p in range(3):
            pick(p, i)
            if p:
                send2(p - 1, i)
        send2(2, i)

    place = ((0, 1, 2), (2, 0, 1), (1, 2, 0))

    def landing(p, s1, s2, s_core):
        lo, n, left, lanes = PARTS[p]
        idx = [None, None, None]
        idx[p] = slice(None)
        idx[(p + 1) % 3] = s1
        idx[(p + 2) % 3] = s2
        return in_ref.at[idx[0], idx[1], idx[2], s_core, pl.ds(lo, n), pl.ds(left, lanes)]

    def p3_copy(p, j, k, flip):
        d1, d2 = (p + 1) % 3, (p + 2) % 3
        src = stage[p].at[0, k, lax.rem(core + flip, 2)] if j == 0 else relay[p].at[j - 1, k, lax.rem(core + flip, 2)]
        s1 = lax.rem(co[d1] + j, 4)
        dst = landing(p, s1, co[d2], core)
        if k == 0 and flip == 0:
            return pltpu.make_async_copy(src, dst, local_sem.at[p * 4 + j])
        return remote(src, dst, p3_send.at[p, j, k * 2 + flip], p3_recv.at[p, j, k * 2 + flip], to(moved(co, d2, k), lax.rem(core + flip, 2)))

    def send3(p, j):
        for k in (1, 3, 2, 0):
            for flip in (0, 1):
                p3_copy(p, j, k, flip).start()

    def finish(j):
        for p in range(3):
            for i in range(4):
                p2_wait(p2_recv, relay, p, i, j - 1)
            send3(p, j)

    def own_pass():
        for p in range(3):
            assemble(p, 0, (1, 3, 2, 0))
            if p:
                send2(p - 1, 0)
        send2(2, 0)

    if fused:
        sums = HubSum(co, core, remote, to, given["u_ref"], *given["sum_refs"])
        sums_in(STEPS)
        sums.start(0)
        weights()
        first_ref, second_ref = given["first_ref"], given["second_ref"]
        size = 4096 // CH
        for q in range(CH):
            sums_in(q)
            update_rows(given["u_ref"], x_ref, q, size, first_ref, second_ref, given["hidden_ref"], given["normed_ref"])
            if q == 2:
                sums.start(1)
            if q == 6:
                sums.start(2)
            if q >= 1:
                ag_start(q - 1)
            if q == 1:
                sums.wait(0)
                sums.add(0)
            if q == 5:
                sums.wait(1)
                sums.add(1)
            if q >= 4:
                relay_on(q - 4)
        assemble(0, 0, (1, 3, 2, 0))
        ag_start(CH - 1)
        relay_on(CH - 4)
        assemble(1, 0, (1, 3, 2, 0))
        sums.wait(2)
        sums.add(2)
        relay_on(CH - 3)
        assemble(2, 0, (1, 3, 2, 0))
        sums.start(3)
        relay_on(CH - 2)
        for p in range(3):
            send2(p, 0)
        relay_on(CH - 1)
        pick(0, 1)
        pick(1, 1)
        pick(2, 1)
        sums.wait(3)
        gathered[co[0], co[1], co[2], core] = feed_forward(sums.result(), first_ref, second_ref)
        pick(0, 3)
        hub_start(0)
        for p in range(3):
            send2(p, 1)
        pick(1, 3)
        send2(0, 3)
        pick(2, 3)
        send2(1, 3)
        send2(2, 3)
        pass_on(2)
        hub_wait(0)
        hub_start(1)
        for p in range(3):
            send3(p, 0)
        finish(1)
        finish(3)
        hub_wait(1)
        hub_start(2)
        finish(2)
        hub_wait(2)
        hub_start(3)
    else:
        for dim in range(3):
            for off in (1, 2, 3):
                list_copy(dim, off).start()
        hub_own = pltpu.make_async_copy(hub_ref, gathered.at[co[0], co[1], co[2], core], local_sem.at[1])
        hub_own.start()
        hub_own.wait()
        hub_start(0)
        for q in range(CH):
            ag_start(q)
        own = pltpu.make_async_copy(list_ref, near_ref.at[pl.ds(0, 1)], local_sem.at[0])
        own.start()
        own.wait()
        for dim in range(3):
            for off in (1, 2, 3):
                list_copy(dim, off).wait_recv()
        fetch = pltpu.make_async_copy(near_ref, lists, smem_sem)
        fetch.start()
        fetch.wait()
        own_pass()
        hub_wait(0)
        hub_start(1)
        for q in range(CH):
            relay_on(q)
        hub_wait(1)
        hub_start(2)
        pass_on(1)
        pass_on(3)
        hub_wait(2)
        hub_start(3)
        pass_on(2)
        for p in range(3):
            send3(p, 0)
        for j in (1, 3, 2):
            finish(j)
    hub_wait(3)
    if not fused:
        wide, ordered = given["wide"], given["ordered"]
        wide[...] = gathered[...].astype(jnp.float32).reshape(wide.shape)

        def rows8(g, carry):
            for r in range(8):
                ordered[pl.ds(g * 8 + r, 1), :] = wide[pl.ds(place_ref[g * 8 + r], 1), :]
            return carry

        lax.fori_loop(0, wide.shape[0] // 8, rows8, 0)
        hubs_ref[...] = ordered[...].astype(jnp.bfloat16)
    else:
        hubs_ref[...] = gathered[...].reshape(hubs_ref.shape)
    for p in range(3):
        for j in range(4):
            for k in range(4):
                for flip in (0, 1):
                    if k == 0 and flip == 0:
                        p3_copy(p, j, k, flip).wait()
                    else:
                        p3_copy(p, j, k, flip).wait()
    for p in range(3):
        for q in range(CH):
            ag_copy(p, q, 0).wait_send()
            ag_copy(p, q, 1).wait_send()
            relay_copy(p, q).wait_send()
        for i in range(4):
            for j in (1, 2, 3):
                p2_copy(p, i, j).wait_send()
    if not fused:
        for dim in range(3):
            for off in (1, 2, 3):
                list_copy(dim, off).wait_send()


def ag_wait(sem, tabs, p, q, slot, per):
    ref = tabs[p][slot].at[pl.ds(q * per, per)]
    pltpu.make_async_copy(ref, ref, sem.at[p, q, slot]).wait()


def p2_wait(sem, relay, p, i, slot):
    ref = relay[p].at[slot, :, :, 0]
    pltpu.make_async_copy(ref, ref, sem.at[p, i, slot]).wait()


STEPS = 8


def load_sums(far_ref, part_ref, u_ref, sem):
    rows = 128 // STEPS
    copies = [pltpu.make_async_copy(far_ref.at[pl.ds(64 + q * rows, rows)], u_ref.at[pl.ds(64 + q * rows, rows)], sem.at[q]) for q in range(STEPS)]
    copies.append(pltpu.make_async_copy(part_ref.at[pl.ds(0, 64)], u_ref.at[pl.ds(0, 64)], sem.at[STEPS]))
    copies[0].start()
    copies[STEPS].start()
    for q in range(1, STEPS):
        copies[q].start()
    return lambda q: copies[q].wait()


def load_weights(w1_ref, w2_ref, first_ref, second_ref, sem, layer):
    copies = [
        pltpu.make_async_copy(w1_ref.at[layer], first_ref, sem.at[0]),
        pltpu.make_async_copy(w2_ref.at[layer], second_ref, sem.at[1]),
    ]
    for copy in copies:
        copy.start()

    def wait():
        for copy in copies:
            copy.wait()

    return wait


class HubSum:
    orders = ((0, 1, 2), (1, 2, 0))

    def __init__(self, co, core, remote, to, part, b0, a0, b1a, b1b, a1, b2a, b2b, a2, b3, send, recv):
        self.co, self.core, self.remote, self.to, self.part = co, core, remote, to, part
        self.b0, self.a0, self.a1, self.a2 = b0, a0, a1, a2
        self.came = ((b1a, b1b), (b2a, b2b), (b3.at[0], b3.at[1]))
        self.b3, self.send, self.recv = b3, send, recv

    def source(self, step, p, at):
        if step == 1:
            rows = pl.ds(p * 8, 8)
            return self.a0.at[at, :, :, rows] if p == 0 else self.a0.at[:, at, :, rows]
        if step == 2:
            return self.a1.at[p, at] if p == 0 else self.a1.at[p, :, at]
        return self.a2.at[p, at]

    def copies(self, step):
        if step == 0:
            return [self.remote(self.part.at[0:64, 1 - self.core], self.b0, self.send.at[0, 0, 0], self.recv.at[0, 0, 0], self.to(self.co, 1 - self.core))]
        out = []
        for p, order in enumerate(self.orders):
            dim = order[step - 1]
            for off in (1, 2, 3):
                src = self.source(step, p, lax.rem(self.co[dim] + off, 4))
                out.append(self.remote(src, self.came[step - 1][p].at[3 - off], self.send.at[step, p, off - 1], self.recv.at[step, p, 3 - off], self.to(moved(self.co, dim, off), self.core)))
        return out

    def start(self, step):
        for copy in self.copies(step):
            copy.start()

    def wait(self, step):
        for copy in self.copies(step):
            copy.wait()

    def add(self, step):
        if step == 0:

            def add0(i, carry):
                self.a0[i] = (self.part[pl.ds(i * 16, 16), self.core] + self.b0[pl.ds(i * 16, 16)]).reshape(4, 4, 16, 256)
                return carry

            lax.fori_loop(0, 4, add0, 0)
            return
        held = self.a1 if step == 1 else self.a2
        for p, order in enumerate(self.orders):
            came = self.came[step - 1][p]
            at = self.co[order[step - 1]]
            if step == 1:
                own = self.a0[at, :, :, p * 8 : p * 8 + 8] if p == 0 else self.a0[:, at, :, p * 8 : p * 8 + 8]
            else:
                own = self.a1[p, at] if p == 0 else self.a1[p, :, at]
            held[p] = own + came[0] + came[1] + came[2]

    def result(self):
        rows = []
        for p, order in enumerate(self.orders):
            rows.append(self.a2[p, self.co[order[2]]] + self.b3[p, 0] + self.b3[p, 1] + self.b3[p, 2])
        return jnp.concatenate(rows, axis=0)


def sum_scratch():
    W, f32, D = pltpu.VMEM, jnp.float32, pltpu.SemaphoreType.DMA
    return [
        W((64, 16, 256), f32), W((4, 4, 4, 16, 256), f32),
        W((3, 4, 4, 8, 256), f32), W((3, 4, 4, 8, 256), f32), W((2, 4, 4, 8, 256), f32),
        W((3, 4, 8, 256), f32), W((3, 4, 8, 256), f32), W((2, 4, 8, 256), f32),
        W((2, 3, 8, 256), f32), D((4, 2, 3)), D((4, 2, 3)),
    ]


def weight_scratch(size):
    bf = jnp.bfloat16
    return [pltpu.VMEM((192, 2, 16, 256), jnp.float32), pltpu.SemaphoreType.DMA((STEPS + 1,)), pltpu.VMEM((256, 2048), bf), pltpu.VMEM((2048, 256), bf), pltpu.VMEM((size, 2048), bf), pltpu.VMEM((size, 256), bf), pltpu.SemaphoreType.DMA((2,))]


def update_rows(u_ref, x_ref, q, size, first, second, hidden_ref, normed_ref):
    def united():
        return u_ref[pl.ds(64 + q * (size // 32), size // 32)].reshape(size, 256)

    u = united()
    normed_ref[...] = (u * lax.rsqrt(jnp.mean(u * u, axis=-1, keepdims=True) + epsilon)).astype(jnp.bfloat16)
    for n in range(0, 2048, 256):
        value = jnp.dot(normed_ref[...], first[:, n : n + 256], preferred_element_type=jnp.float32)
        hidden_ref[:, n : n + 256] = jnp.maximum(value, 0.0).astype(jnp.bfloat16)
    total = united() + jnp.dot(hidden_ref[...], second[...], preferred_element_type=jnp.float32)
    x_ref[pl.ds(q * (size // 128), size // 128)] = total.astype(jnp.bfloat16).reshape(size // 128, 128, 256)


def route_scratch(chunks):
    bf, D = jnp.bfloat16, pltpu.SemaphoreType.DMA
    scratch = [pltpu.VMEM((4, 4, 4, 2, 16, 256), bf)]
    scratch += [pltpu.VMEM((32, n, w), bf) for lo, n, left, w in PARTS for _ in range(3)]
    scratch += [pltpu.VMEM((4, 4, 2, 4, n, w), bf) for lo, n, left, w in PARTS]
    scratch += [pltpu.VMEM((3, 4, 2, 4, n, w), bf) for lo, n, left, w in PARTS]
    scratch += [D((3, 4)), D((3, 4)), D, D((3, chunks, 3)), D((3, chunks, 3)), D((3, 4, 3)), D((3, 4, 3)), D((3, 4, 8)), D((3, 4, 8)), D((12,))]
    return scratch + [D((4, 6)), D((4, 6))]


def exchange(x, send_list, hubs, place):
    bf, f32 = jnp.bfloat16, jnp.float32
    V = pl.BlockSpec(memory_space=pltpu.VMEM)
    return pl.pallas_call(
        functools.partial(exchange_kernel, False, 4),
        out_shape=(
            jax.ShapeDtypeStruct((4, 4, 4, 2, 128, 256), bf),
            jax.ShapeDtypeStruct((2048, 256), bf),
            jax.ShapeDtypeStruct((12, 128), jnp.int32),
        ),
        in_specs=[V, V, V, pl.BlockSpec(memory_space=pltpu.SMEM)],
        out_specs=(pl.BlockSpec(memory_space=pltpu.HBM), V, V),
        scratch_shapes=[pltpu.SMEM((12, 128), jnp.int32), pltpu.VMEM((2048, 256), f32), pltpu.VMEM((2048, 256), f32)] + route_scratch(4),
        compiler_params=pltpu.CompilerParams(collective_id=0, has_side_effects=True, vmem_limit_bytes=60 * 2**20),
        name="exchange",
    )(x, send_list, hubs, place)


def update_exchange(u, near, w_in, w_out):
    bf = jnp.bfloat16
    V, A = pl.BlockSpec(memory_space=pltpu.VMEM), pl.BlockSpec(memory_space=pl.ANY)
    return pl.pallas_call(
        functools.partial(exchange_kernel, True, 8),
        out_shape=(
            jax.ShapeDtypeStruct((4, 4, 4, 2, 128, 256), bf),
            jax.ShapeDtypeStruct((2048, 256), bf),
            jax.ShapeDtypeStruct((32, 128, 256), bf),
        ),
        in_specs=[A, pl.BlockSpec(memory_space=pltpu.SMEM), A, A],
        out_specs=(pl.BlockSpec(memory_space=pltpu.HBM), V, V),
        scratch_shapes=weight_scratch(512) + sum_scratch() + route_scratch(8),
        compiler_params=pltpu.CompilerParams(collective_id=1, has_side_effects=True, vmem_limit_bytes=60 * 2**20),
        name="update_exchange",
    )(u.reshape(192, 2, 16, 256), near, w_in, w_out)


GROUP = 64
BATCH = 16


def tiles_kernel(last, rows_ref, cols_ref, count_ref, place_ref, tiles_ref, x_ref, hubs_ref, in_ref, out_ref, *rest):
    group = pl.program_id(0)
    hub_count, own_count, remote_groups = 16, 32, 128 // GROUP
    table = rest[-1]
    count = count_ref[0]
    position = lax.axis_index("dev")

    def near(block):
        return jnp.where(block < hub_count, block, block - position * own_count)

    @pl.when(group == 0)
    def _():
        def hub(b, carry):
            block = hubs_ref[b]
            out_ref[b] = jnp.where(position == 0, block.astype(jnp.float32), 0.0)
            table[b] = block
            return carry

        lax.fori_loop(0, hub_count, hub, 0)

        def own(b, carry):
            block = x_ref[b]
            out_ref[hub_count + b] = block.astype(jnp.float32)
            table[hub_count + b] = block
            return carry

        lax.fori_loop(0, own_count, own, 0)

    def add(items):
        products = [jnp.dot(tile, block, preferred_element_type=jnp.float32) for slot, tile, block in items]
        for (slot, tile, block), product in zip(items, products):
            row = near(rows_ref[slot])
            out_ref[row] = out_ref[row] + product

    live = jnp.clip(count - group * GROUP, 0, GROUP)

    @pl.when(group < remote_groups)
    def _():
        def step(t, carry):
            add([(group * GROUP + t * BATCH + s, tiles_ref[t * BATCH + s], in_ref[t * BATCH + s]) for s in range(BATCH)])
            return carry

        lax.fori_loop(0, GROUP // BATCH, step, 0)

    @pl.when(group >= remote_groups)
    def _():
        def local(s):
            slot = group * GROUP + s
            return slot, tiles_ref[s], table[near(cols_ref[slot - 128])]

        def step(t, carry):
            add([local(t * BATCH + s) for s in range(BATCH)])
            return carry

        full = live // BATCH
        lax.fori_loop(0, full, step, 0)
        lax.fori_loop(full * BATCH, live, lambda s, carry: (add([local(s)]), carry)[1], 0)

    if last:
        perm_ref = rest[0]

        @pl.when(group == pl.num_programs(0) - 1)
        def _():
            def rows32(g, carry):
                block = out_ref[g // 4, pl.ds(lax.rem(g, 4) * 32, 32), :]
                for r in range(32):
                    perm_ref[pl.ds(place_ref[g * 32 + r], 1), :] = block[r : r + 1]
                return carry

            lax.fori_loop(0, place_ref.shape[0] // 32, rows32, 0)


def sum_tiles(last, rows, cols, count, place, tiles, x, hubs, landed):
    capacity = tiles.shape[0]
    f32 = jnp.float32
    groups = -(-capacity // GROUP)

    def full(*shape):
        return pl.BlockSpec(shape, lambda g, *s: (0,) * len(shape))

    out_shape = [jax.ShapeDtypeStruct((48, 128, 256), f32)]
    out_specs = [full(48, 128, 256)]
    if last:
        out_shape.append(jax.ShapeDtypeStruct((2048, 256), f32))
        out_specs.append(full(2048, 256))
    return pl.pallas_call(
        functools.partial(tiles_kernel, last),
        grid_spec=pltpu.PrefetchScalarGridSpec(
            num_scalar_prefetch=4,
            grid=(groups,),
            in_specs=[
                pl.BlockSpec((GROUP, 128, 128), lambda g, rows, cols, count, place: (jnp.minimum(g, (count[0] - 1) // GROUP), 0, 0)),
                full(32, 128, 256),
                full(16, 128, 256),
                pl.BlockSpec((GROUP, 128, 256), lambda g, *s: (jnp.minimum(g, 128 // GROUP - 1), 0, 0)),
            ],
            out_specs=out_specs,
            scratch_shapes=[pltpu.VMEM((48, 128, 256), jnp.bfloat16)],
        ),
        out_shape=out_shape,
        compiler_params=pltpu.CompilerParams(dimension_semantics=("arbitrary",), vmem_limit_bytes=60 * 2**20),
        name="sum_tiles",
    )(rows, cols, count, place, tiles, x, hubs.reshape(16, 128, 256), landed.reshape(128, 128, 256))


def feed_forward(united, first, second):
    scale = lax.rsqrt(jnp.mean(united * united, axis=-1, keepdims=True) + epsilon)
    normed = (united * scale).astype(jnp.bfloat16)
    total = united
    step = 512
    for n in range(0, first.shape[1], step):
        hidden = jnp.dot(normed, first[:, n : n + step], preferred_element_type=jnp.float32)
        hidden = jnp.maximum(hidden, 0.0).astype(jnp.bfloat16)
        total = total + jnp.dot(hidden, second[n : n + step, :], preferred_element_type=jnp.float32)
    return total.astype(jnp.bfloat16)


def update_kernel(far_ref, part_ref, w1_ref, w2_ref, out_ref, hub_out_ref, u_ref, u_sem, first_ref, second_ref, hidden_ref, normed_ref, w_sem, *sum_refs):
    sums_in = load_sums(far_ref, part_ref, u_ref, u_sem)
    weights = load_weights(w1_ref, w2_ref, first_ref, second_ref, w_sem, 1)
    co, core = coords()

    def to(co2, core2):
        return (device_of(co2, core2),)

    bar = pltpu.get_barrier_semaphore()
    pl.semaphore_signal(bar, inc=1, device_id=to(co, 1 - core), device_id_type=MESH)
    for dim in range(3):
        for off in (1, 2, 3):
            pl.semaphore_signal(bar, inc=1, device_id=to(moved(co, dim, off), core), device_id_type=MESH)
    pl.semaphore_wait(bar, 10)

    def remote(src, dst, ssem, rsem, dev):
        return pltpu.make_async_remote_copy(src_ref=src, dst_ref=dst, send_sem=ssem, recv_sem=rsem, device_id=dev, device_id_type=MESH)

    sums = HubSum(co, core, remote, to, u_ref, *sum_refs)
    sums_in(STEPS)
    sums.start(0)
    weights()
    size = hidden_ref.shape[0]
    for q in range(STEPS):
        sums_in(q)
        update_rows(u_ref, out_ref, q, size, first_ref, second_ref, hidden_ref, normed_ref)
        if q == 0:
            sums.wait(0)
            sums.add(0)
        if q == 1:
            sums.start(1)
        if q == 5:
            sums.wait(1)
            sums.add(1)
        if q == 6:
            sums.start(2)
    sums.wait(2)
    sums.add(2)
    sums.start(3)
    sums.wait(3)
    hub_out_ref[...] = feed_forward(sums.result(), first_ref, second_ref)


def update(u, part, w_in, w_out):
    bf = jnp.bfloat16
    V, A = pl.BlockSpec(memory_space=pltpu.VMEM), pl.BlockSpec(memory_space=pl.ANY)
    return pl.pallas_call(
        update_kernel,
        out_shape=(jax.ShapeDtypeStruct((32, 128, 256), bf), jax.ShapeDtypeStruct((16, 256), bf)),
        in_specs=[A, A, A, A],
        out_specs=(V, V),
        scratch_shapes=weight_scratch(512) + sum_scratch(),
        compiler_params=pltpu.CompilerParams(collective_id=2, has_side_effects=True, vmem_limit_bytes=60 * 2**20),
        name="update",
    )(u.reshape(192, 2, 16, 256), part.reshape(-1, 2, 16, 256), w_in, w_out)


def body(peripheral, hubs, tiles, tile_rows, local_cols, tile_count, send_list, hub_place, w_in, w_out):
    x = peripheral.reshape(-1, 128, 256)
    landed, table, near = exchange(x, send_list, hubs, hub_place)
    (u,) = sum_tiles(False, tile_rows, local_cols, tile_count, hub_place, tiles, x, table, landed)
    landed, table, x = update_exchange(u, near, w_in, w_out)
    u, part = sum_tiles(True, tile_rows, local_cols, tile_count, hub_place, tiles, x, table, landed)
    new, hub_new = update(u, part, w_in, w_out)
    return new.reshape(peripheral.shape), hub_new


def solution(mesh):
    split = P("dev")
    in_specs = (split, split, split, split, split, split, split, P(), P(), P())
    return jax.shard_map(body, mesh=mesh, in_specs=in_specs, out_specs=(split, split), check_vma=False)
```

```python
import functools
import jax
import jax.numpy as jnp
from jax import lax
from jax.sharding import PartitionSpec as P
from jax.experimental import pallas as pl
from jax.experimental.pallas import tpu as pltpu

MESH = pl.DeviceIdType.MESH
PARTS = ((0, 88, 0, 128), (0, 88, 128, 128), (88, 40, 0, 256))
epsilon = 1e-06


def coords():
    me = lax.axis_index("dev")
    return [me // 32, lax.rem(me // 8, 4), lax.rem(me // 2, 4)], lax.rem(me, 2)


def device_of(co, core):
    return ((co[0] * 4 + co[1]) * 4 + co[2]) * 2 + core


def moved(co, dim, off):
    out = list(co)
    out[dim] = lax.rem(co[dim] + off, 4)
    return out


def exchange_kernel(fused, CH, *refs):
    if fused:
        far_ref, lists, w1_ref, w2_ref, in_ref, hubs_ref, x_ref = refs[:7]
        u_ref, u_sem, first_ref, second_ref, hidden_ref, normed_ref, w_sem = refs[7:14]
        sum_refs = refs[14:25]
        refs = refs[25:]
    else:
        x_ref, list_ref, hub_ref, place_ref, in_ref, hubs_ref, near_ref, lists, wide, ordered = refs[:10]
        refs = refs[10:]
    exchange_steps(fused, CH, locals(), *refs)


def exchange_steps(fused, CH, given, gathered, t00, t01, t02, t10, t11, t12, t20, t21, t22, s0, s1, s2, r0, r1, r2,
                    list_sem, list_send, smem_sem, ag_send, ag_recv, p2_send, p2_recv, p3_send, p3_recv, local_sem, hub_send, hub_recv):
    x_ref, in_ref, hubs_ref, lists = given["x_ref"], given["in_ref"], given["hubs_ref"], given["lists"]
    if fused:
        sums_in = load_sums(given["far_ref"], given["far_ref"], given["u_ref"], given["u_sem"])
        weights = load_weights(given["w1_ref"], given["w2_ref"], given["first_ref"], given["second_ref"], given["w_sem"], 0)
    else:
        list_ref, hub_ref, place_ref, near_ref = given["list_ref"], given["hub_ref"], given["place_ref"], given["near_ref"]
    tabs = ((t00, t01, t02), (t10, t11, t12), (t20, t21, t22))
    stage, relay = (s0, s1, s2), (r0, r1, r2)
    co, core = coords()
    blocks = x_ref.shape[0]
    per = blocks // CH

    def to(co2, core2):
        return (device_of(co2, core2),)

    bar = pltpu.get_barrier_semaphore()
    for dim in range(3):
        for off in (1, 2, 3):
            for flip in (0, 1):
                pl.semaphore_signal(bar, inc=1, device_id=to(moved(co, dim, off), lax.rem(core + flip, 2)), device_id_type=MESH)
    pl.semaphore_signal(bar, inc=1, device_id=to(co, 1 - core), device_id_type=MESH)
    pl.semaphore_wait(bar, 19)

    def remote(src, dst, ssem, rsem, dev):
        return pltpu.make_async_remote_copy(src_ref=src, dst_ref=dst, send_sem=ssem, recv_sem=rsem, device_id=dev, device_id_type=MESH)

    def list_copy(dim, off):
        return remote(list_ref, near_ref.at[pl.ds(dim * 4 + 4 - off, 1)], list_send.at[dim, off], list_sem.at[dim, 4 - off], to(moved(co, dim, off), core))

    def hub_copy(step, off):
        if step == 3:
            part = gathered.at[:, :, :, core]
            return remote(part, part, hub_send.at[3, 0], hub_recv.at[3, 0], to(co, 1 - core))
        half, off = off // 4, off % 4
        rows = pl.ds(half * 8, 8)
        dim = ((2, 1, 0), (0, 2, 1))[half][step]
        x, y, z = co
        every = slice(None)
        at = (((x, y, z), (x, y, every), (x, every, every)), ((x, y, z), (every, y, z), (every, y, every)))[half][step]
        part = gathered.at[at[0], at[1], at[2], core, rows]
        return remote(part, part, hub_send.at[step, half * 3 + off - 1], hub_recv.at[step, half * 3 + 3 - off], to(moved(co, dim, off), core))

    def hub_start(step):
        for off in (1, 2, 3, 5, 6, 7) if step < 3 else (1,):
            hub_copy(step, off).start()

    def hub_wait(step):
        for off in (1, 2, 3, 5, 6, 7) if step < 3 else (1,):
            hub_copy(step, off).wait()

    def ag_copy(p, q, direction):
        lo, n, left, lanes = PARTS[p]
        off = 1 if direction == 0 else 3
        seen = 4 - off
        return remote(x_ref.at[pl.ds(q * per, per), pl.ds(lo, n), pl.ds(left, lanes)], tabs[p][seen - 1].at[pl.ds(q * per, per)],
                      ag_send.at[p, q, direction], ag_recv.at[p, q, seen - 1], to(moved(co, p, off), core))

    def relay_copy(p, q):
        off = 1 if q % 2 == 0 else 3
        seen = 4 - off
        return remote(tabs[p][seen - 1].at[pl.ds(q * per, per)], tabs[p][1].at[pl.ds(q * per, per)],
                      ag_send.at[p, q, 2], ag_recv.at[p, q, 1], to(moved(co, p, off), core))

    def ag_start(q):
        for p in range(3):
            for direction in (0, 1) if q % 2 == 0 else (1, 0):
                ag_copy(p, q, direction).start()

    def relay_on(q):
        for p in range(3):
            ag_wait(ag_recv, tabs, p, q, 2 if q % 2 == 0 else 0, per)
            relay_copy(p, q).start()

    def assemble(p, i, js):
        lo, n, left, lanes = PARTS[p]
        d1, d2 = (p + 1) % 3, (p + 2) % 3
        where = lax.rem(co[p] + i, 4)
        row = 0 if i == 0 else p * 4 + i
        for j in js:
            def piece(m, carry, j=j):
                k, flip = m // 2, lax.rem(m, 2)
                target = device_of(moved(moved(co, d1, j), d2, k), flip)
                b = lists[row, target]
                value = x_ref[b, lo:lo + n, left:left + lanes] if i == 0 else tabs[p][i - 1][b]
                stage[p][j, k, flip, where] = value
                return carry
            lax.fori_loop(0, 8, piece, 0)

    def p2_copy(p, i, j):
        d1 = (p + 1) % 3
        where = lax.rem(co[p] + i, 4)
        return remote(stage[p].at[j, :, :, where], relay[p].at[3 - j, :, :, where],
                      p2_send.at[p, i, j - 1], p2_recv.at[p, i, 3 - j], to(moved(co, d1, j), core))

    def send2(p, i):
        for j in (1, 3, 2):
            p2_copy(p, i, j).start()

    def pick(p, i):
        for q in range(CH):
            if i == 2 or (i == 1 and q % 2 == 0) or (i == 3 and q % 2 == 1):
                ag_wait(ag_recv, tabs, p, q, i - 1, per)
        assemble(p, i, (1, 3, 2, 0))

    def pass_on(i):
        for p in range(3):
            pick(p, i)
            if p:
                send2(p - 1, i)
        send2(2, i)

    place = ((0, 1, 2), (2, 0, 1), (1, 2, 0))

    def landing(p, s1, s2, s_core):
        lo, n, left, lanes = PARTS[p]
        idx = [None, None, None]
        idx[p] = slice(None)
        idx[(p + 1) % 3] = s1
        idx[(p + 2) % 3] = s2
        return in_ref.at[idx[0], idx[1], idx[2], s_core, pl.ds(lo, n), pl.ds(left, lanes)]

    def p3_copy(p, j, k, flip):
        d1, d2 = (p + 1) % 3, (p + 2) % 3
        src = stage[p].at[0, k, lax.rem(core + flip, 2)] if j == 0 else relay[p].at[j - 1, k, lax.rem(core + flip, 2)]
        s1 = lax.rem(co[d1] + j, 4)
        dst = landing(p, s1, co[d2], core)
        if k == 0 and flip == 0:
            return pltpu.make_async_copy(src, dst, local_sem.at[p * 4 + j])
        return remote(src, dst, p3_send.at[p, j, k * 2 + flip], p3_recv.at[p, j, k * 2 + flip], to(moved(co, d2, k), lax.rem(core + flip, 2)))

    def send3(p, j):
        for k in (1, 3, 2, 0):
            for flip in (0, 1):
                p3_copy(p, j, k, flip).start()

    def finish(j):
        for p in range(3):
            for i in range(4):
                p2_wait(p2_recv, relay, p, i, j - 1)
            send3(p, j)

    def own_pass():
        for p in range(3):
            assemble(p, 0, (1, 3, 2, 0))
            if p:
                send2(p - 1, 0)
        send2(2, 0)

    if fused:
        sums = HubSum(co, core, remote, to, given["u_ref"], *given["sum_refs"])
        sums_in(STEPS)
        sums.start(0)
        weights()
        first_ref, second_ref = given["first_ref"], given["second_ref"]
        size = 4096 // CH
        for q in range(CH):
            sums_in(q)
            update_rows(given["u_ref"], x_ref, q, size, first_ref, second_ref, given["hidden_ref"], given["normed_ref"])
            if q == 2:
                sums.start(1)
            if q == 6:
                sums.start(2)
            if q >= 1:
                ag_start(q - 1)
            if q == 1:
                sums.wait(0)
                sums.add(0)
            if q == 5:
                sums.wait(1)
                sums.add(1)
            if q >= 4:
                relay_on(q - 4)
        assemble(0, 0, (1, 3, 2, 0))
        ag_start(CH - 1)
        relay_on(CH - 4)
        assemble(1, 0, (1, 3, 2, 0))
        sums.wait(2)
        sums.add(2)
        relay_on(CH - 3)
        assemble(2, 0, (1, 3, 2, 0))
        sums.start(3)
        relay_on(CH - 2)
        for p in range(3):
            send2(p, 0)
        relay_on(CH - 1)
        pick(0, 1)
        pick(1, 1)
        pick(2, 1)
        sums.wait(3)
        gathered[co[0], co[1], co[2], core] = feed_forward(sums.result(), first_ref, second_ref)
        pick(0, 3)
        hub_start(0)
        for p in range(3):
            send2(p, 1)
        pick(1, 3)
        send2(0, 3)
        pick(2, 3)
        send2(1, 3)
        send2(2, 3)
        pass_on(2)
        hub_wait(0)
        hub_start(1)
        for p in range(3):
            send3(p, 0)
        finish(1)
        finish(3)
        hub_wait(1)
        hub_start(2)
        finish(2)
        hub_wait(2)
        hub_start(3)
    else:
        for dim in range(3):
            for off in (1, 2, 3):
                list_copy(dim, off).start()
        hub_own = pltpu.make_async_copy(hub_ref, gathered.at[co[0], co[1], co[2], core], local_sem.at[1])
        hub_own.start()
        hub_own.wait()
        hub_start(0)
        for q in range(CH):
            ag_start(q)
        own = pltpu.make_async_copy(list_ref, near_ref.at[pl.ds(0, 1)], local_sem.at[0])
        own.start()
        own.wait()
        for dim in range(3):
            for off in (1, 2, 3):
                list_copy(dim, off).wait_recv()
        fetch = pltpu.make_async_copy(near_ref, lists, smem_sem)
        fetch.start()
        fetch.wait()
        own_pass()
        hub_wait(0)
        hub_start(1)
        for q in range(CH):
            relay_on(q)
        hub_wait(1)
        hub_start(2)
        pass_on(1)
        pass_on(3)
        hub_wait(2)
        hub_start(3)
        pass_on(2)
        for p in range(3):
            send3(p, 0)
        for j in (1, 3, 2):
            finish(j)
    hub_wait(3)
    if not fused:
        wide, ordered = given["wide"], given["ordered"]
        wide[...] = gathered[...].astype(jnp.float32).reshape(wide.shape)

        def rows8(g, carry):
            for r in range(8):
                ordered[pl.ds(g * 8 + r, 1), :] = wide[pl.ds(place_ref[g * 8 + r], 1), :]
            return carry

        lax.fori_loop(0, wide.shape[0] // 8, rows8, 0)
        hubs_ref[...] = ordered[...].astype(jnp.bfloat16)
    else:
        hubs_ref[...] = gathered[...].reshape(hubs_ref.shape)
    for p in range(3):
        for j in range(4):
            for k in range(4):
                for flip in (0, 1):
                    if k == 0 and flip == 0:
                        p3_copy(p, j, k, flip).wait()
                    else:
                        p3_copy(p, j, k, flip).wait()
    for p in range(3):
        for q in range(CH):
            ag_copy(p, q, 0).wait_send()
            ag_copy(p, q, 1).wait_send()
            relay_copy(p, q).wait_send()
        for i in range(4):
            for j in (1, 2, 3):
                p2_copy(p, i, j).wait_send()
    if not fused:
        for dim in range(3):
            for off in (1, 2, 3):
                list_copy(dim, off).wait_send()


def ag_wait(sem, tabs, p, q, slot, per):
    ref = tabs[p][slot].at[pl.ds(q * per, per)]
    pltpu.make_async_copy(ref, ref, sem.at[p, q, slot]).wait()


def p2_wait(sem, relay, p, i, slot):
    ref = relay[p].at[slot, :, :, 0]
    pltpu.make_async_copy(ref, ref, sem.at[p, i, slot]).wait()


STEPS = 8


def load_sums(far_ref, part_ref, u_ref, sem):
    rows = 128 // STEPS
    copies = [pltpu.make_async_copy(far_ref.at[pl.ds(64 + q * rows, rows)], u_ref.at[pl.ds(64 + q * rows, rows)], sem.at[q]) for q in range(STEPS)]
    copies.append(pltpu.make_async_copy(part_ref.at[pl.ds(0, 64)], u_ref.at[pl.ds(0, 64)], sem.at[STEPS]))
    copies[0].start()
    copies[STEPS].start()
    for q in range(1, STEPS):
        copies[q].start()
    return lambda q: copies[q].wait()


def load_weights(w1_ref, w2_ref, first_ref, second_ref, sem, layer):
    copies = [
        pltpu.make_async_copy(w1_ref.at[layer], first_ref, sem.at[0]),
        pltpu.make_async_copy(w2_ref.at[layer], second_ref, sem.at[1]),
    ]
    for copy in copies:
        copy.start()

    def wait():
        for copy in copies:
            copy.wait()

    return wait


class HubSum:
    orders = ((0, 1, 2), (1, 2, 0))

    def __init__(self, co, core, remote, to, part, b0, a0, b1a, b1b, a1, b2a, b2b, a2, b3, send, recv):
        self.co, self.core, self.remote, self.to, self.part = co, core, remote, to, part
        self.b0, self.a0, self.a1, self.a2 = b0, a0, a1, a2
        self.came = ((b1a, b1b), (b2a, b2b), (b3.at[0], b3.at[1]))
        self.b3, self.send, self.recv = b3, send, recv

    def source(self, step, p, at):
        if step == 1:
            rows = pl.ds(p * 8, 8)
            return self.a0.at[at, :, :, rows] if p == 0 else self.a0.at[:, at, :, rows]
        if step == 2:
            return self.a1.at[p, at] if p == 0 else self.a1.at[p, :, at]
        return self.a2.at[p, at]

    def copies(self, step):
        if step == 0:
            return [self.remote(self.part.at[0:64, 1 - self.core], self.b0, self.send.at[0, 0, 0], self.recv.at[0, 0, 0], self.to(self.co, 1 - self.core))]
        out = []
        for p, order in enumerate(self.orders):
            dim = order[step - 1]
            for off in (1, 2, 3):
                src = self.source(step, p, lax.rem(self.co[dim] + off, 4))
                out.append(self.remote(src, self.came[step - 1][p].at[3 - off], self.send.at[step, p, off - 1], self.recv.at[step, p, 3 - off], self.to(moved(self.co, dim, off), self.core)))
        return out

    def start(self, step):
        for copy in self.copies(step):
            copy.start()

    def wait(self, step):
        for copy in self.copies(step):
            copy.wait()

    def add(self, step):
        if step == 0:

            def add0(i, carry):
                self.a0[i] = (self.part[pl.ds(i * 16, 16), self.core] + self.b0[pl.ds(i * 16, 16)]).reshape(4, 4, 16, 256)
                return carry

            lax.fori_loop(0, 4, add0, 0)
            return
        held = self.a1 if step == 1 else self.a2
        for p, order in enumerate(self.orders):
            came = self.came[step - 1][p]
            at = self.co[order[step - 1]]
            if step == 1:
                own = self.a0[at, :, :, p * 8 : p * 8 + 8] if p == 0 else self.a0[:, at, :, p * 8 : p * 8 + 8]
            else:
                own = self.a1[p, at] if p == 0 else self.a1[p, :, at]
            held[p] = own + came[0] + came[1] + came[2]

    def result(self):
        rows = []
        for p, order in enumerate(self.orders):
            rows.append(self.a2[p, self.co[order[2]]] + self.b3[p, 0] + self.b3[p, 1] + self.b3[p, 2])
        return jnp.concatenate(rows, axis=0)


def sum_scratch():
    W, f32, D = pltpu.VMEM, jnp.float32, pltpu.SemaphoreType.DMA
    return [
        W((64, 16, 256), f32), W((4, 4, 4, 16, 256), f32),
        W((3, 4, 4, 8, 256), f32), W((3, 4, 4, 8, 256), f32), W((2, 4, 4, 8, 256), f32),
        W((3, 4, 8, 256), f32), W((3, 4, 8, 256), f32), W((2, 4, 8, 256), f32),
        W((2, 3, 8, 256), f32), D((4, 2, 3)), D((4, 2, 3)),
    ]


def weight_scratch(size):
    bf = jnp.bfloat16
    return [pltpu.VMEM((192, 2, 16, 256), jnp.float32), pltpu.SemaphoreType.DMA((STEPS + 1,)), pltpu.VMEM((256, 2048), bf), pltpu.VMEM((2048, 256), bf), pltpu.VMEM((size, 2048), bf), pltpu.VMEM((size, 256), bf), pltpu.SemaphoreType.DMA((2,))]


def update_rows(u_ref, x_ref, q, size, first, second, hidden_ref, normed_ref):
    def united():
        return u_ref[pl.ds(64 + q * (size // 32), size // 32)].reshape(size, 256)

    u = united()
    normed_ref[...] = (u * lax.rsqrt(jnp.mean(u * u, axis=-1, keepdims=True) + epsilon)).astype(jnp.bfloat16)
    for n in range(0, 2048, 256):
        value = jnp.dot(normed_ref[...], first[:, n : n + 256], preferred_element_type=jnp.float32)
        hidden_ref[:, n : n + 256] = jnp.maximum(value, 0.0).astype(jnp.bfloat16)
    total = united() + jnp.dot(hidden_ref[...], second[...], preferred_element_type=jnp.float32)
    x_ref[pl.ds(q * (size // 128), size // 128)] = total.astype(jnp.bfloat16).reshape(size // 128, 128, 256)


def route_scratch(chunks):
    bf, D = jnp.bfloat16, pltpu.SemaphoreType.DMA
    scratch = [pltpu.VMEM((4, 4, 4, 2, 16, 256), bf)]
    scratch += [pltpu.VMEM((32, n, w), bf) for lo, n, left, w in PARTS for _ in range(3)]
    scratch += [pltpu.VMEM((4, 4, 2, 4, n, w), bf) for lo, n, left, w in PARTS]
    scratch += [pltpu.VMEM((3, 4, 2, 4, n, w), bf) for lo, n, left, w in PARTS]
    scratch += [D((3, 4)), D((3, 4)), D, D((3, chunks, 3)), D((3, chunks, 3)), D((3, 4, 3)), D((3, 4, 3)), D((3, 4, 8)), D((3, 4, 8)), D((12,))]
    return scratch + [D((4, 6)), D((4, 6))]


def exchange(x, send_list, hubs, place):
    bf, f32 = jnp.bfloat16, jnp.float32
    V = pl.BlockSpec(memory_space=pltpu.VMEM)
    return pl.pallas_call(
        functools.partial(exchange_kernel, False, 4),
        out_shape=(
            jax.ShapeDtypeStruct((4, 4, 4, 2, 128, 256), bf),
            jax.ShapeDtypeStruct((2048, 256), bf),
            jax.ShapeDtypeStruct((12, 128), jnp.int32),
        ),
        in_specs=[V, V, V, pl.BlockSpec(memory_space=pltpu.SMEM)],
        out_specs=(pl.BlockSpec(memory_space=pltpu.HBM), V, V),
        scratch_shapes=[pltpu.SMEM((12, 128), jnp.int32), pltpu.VMEM((2048, 256), f32), pltpu.VMEM((2048, 256), f32)] + route_scratch(4),
        compiler_params=pltpu.CompilerParams(collective_id=0, has_side_effects=True, vmem_limit_bytes=60 * 2**20),
        name="exchange",
    )(x, send_list, hubs, place)


def update_exchange(u, near, w_in, w_out):
    bf = jnp.bfloat16
    V, A = pl.BlockSpec(memory_space=pltpu.VMEM), pl.BlockSpec(memory_space=pl.ANY)
    return pl.pallas_call(
        functools.partial(exchange_kernel, True, 8),
        out_shape=(
            jax.ShapeDtypeStruct((4, 4, 4, 2, 128, 256), bf),
            jax.ShapeDtypeStruct((2048, 256), bf),
            jax.ShapeDtypeStruct((32, 128, 256), bf),
        ),
        in_specs=[A, pl.BlockSpec(memory_space=pltpu.SMEM), A, A],
        out_specs=(pl.BlockSpec(memory_space=pltpu.HBM), V, V),
        scratch_shapes=weight_scratch(512) + sum_scratch() + route_scratch(8),
        compiler_params=pltpu.CompilerParams(collective_id=1, has_side_effects=True, vmem_limit_bytes=60 * 2**20),
        name="update_exchange",
    )(u.reshape(192, 2, 16, 256), near, w_in, w_out)


GROUP = 64
BATCH = 16


def tiles_kernel(last, rows_ref, cols_ref, count_ref, place_ref, tiles_ref, x_ref, hubs_ref, in_ref, out_ref, *rest):
    group = pl.program_id(0)
    hub_count, own_count, remote_groups = 16, 32, 128 // GROUP
    table = rest[-1]
    count = count_ref[0]
    position = lax.axis_index("dev")

    def near(block):
        return jnp.where(block < hub_count, block, block - position * own_count)

    @pl.when(group == 0)
    def _():
        def hub(b, carry):
            block = hubs_ref[b]
            out_ref[b] = jnp.where(position == 0, block.astype(jnp.float32), 0.0)
            table[b] = block
            return carry

        lax.fori_loop(0, hub_count, hub, 0)

        def own(b, carry):
            block = x_ref[b]
            out_ref[hub_count + b] = block.astype(jnp.float32)
            table[hub_count + b] = block
            return carry

        lax.fori_loop(0, own_count, own, 0)

    def add(items):
        products = [jnp.dot(tile, block, preferred_element_type=jnp.float32) for slot, tile, block in items]
        for (slot, tile, block), product in zip(items, products):
            row = near(rows_ref[slot])
            out_ref[row] = out_ref[row] + product

    live = jnp.clip(count - group * GROUP, 0, GROUP)

    @pl.when(group < remote_groups)
    def _():
        def step(t, carry):
            add([(group * GROUP + t * BATCH + s, tiles_ref[t * BATCH + s], in_ref[t * BATCH + s]) for s in range(BATCH)])
            return carry

        lax.fori_loop(0, GROUP // BATCH, step, 0)

    @pl.when(group >= remote_groups)
    def _():
        def local(s):
            slot = group * GROUP + s
            return slot, tiles_ref[s], table[near(cols_ref[slot - 128])]

        def step(t, carry):
            add([local(t * BATCH + s) for s in range(BATCH)])
            return carry

        full = live // BATCH
        lax.fori_loop(0, full, step, 0)
        lax.fori_loop(full * BATCH, live, lambda s, carry: (add([local(s)]), carry)[1], 0)

    if last:
        perm_ref = rest[0]

        @pl.when(group == pl.num_programs(0) - 1)
        def _():
            def rows32(g, carry):
                block = out_ref[g // 4, pl.ds(lax.rem(g, 4) * 32, 32), :]
                for r in range(32):
                    perm_ref[pl.ds(place_ref[g * 32 + r], 1), :] = block[r : r + 1]
                return carry

            lax.fori_loop(0, place_ref.shape[0] // 32, rows32, 0)


def sum_tiles(last, rows, cols, count, place, tiles, x, hubs, landed):
    capacity = tiles.shape[0]
    f32 = jnp.float32
    groups = -(-capacity // GROUP)

    def full(*shape):
        return pl.BlockSpec(shape, lambda g, *s: (0,) * len(shape))

    out_shape = [jax.ShapeDtypeStruct((48, 128, 256), f32)]
    out_specs = [full(48, 128, 256)]
    if last:
        out_shape.append(jax.ShapeDtypeStruct((2048, 256), f32))
        out_specs.append(full(2048, 256))
    return pl.pallas_call(
        functools.partial(tiles_kernel, last),
        grid_spec=pltpu.PrefetchScalarGridSpec(
            num_scalar_prefetch=4,
            grid=(groups,),
            in_specs=[
                pl.BlockSpec((GROUP, 128, 128), lambda g, rows, cols, count, place: (jnp.minimum(g, (count[0] - 1) // GROUP), 0, 0)),
                full(32, 128, 256),
                full(16, 128, 256),
                pl.BlockSpec((GROUP, 128, 256), lambda g, *s: (jnp.minimum(g, 128 // GROUP - 1), 0, 0)),
            ],
            out_specs=out_specs,
            scratch_shapes=[pltpu.VMEM((48, 128, 256), jnp.bfloat16)],
        ),
        out_shape=out_shape,
        compiler_params=pltpu.CompilerParams(dimension_semantics=("arbitrary",), vmem_limit_bytes=60 * 2**20),
        name="sum_tiles",
    )(rows, cols, count, place, tiles, x, hubs.reshape(16, 128, 256), landed.reshape(128, 128, 256))


def feed_forward(united, first, second):
    scale = lax.rsqrt(jnp.mean(united * united, axis=-1, keepdims=True) + epsilon)
    normed = (united * scale).astype(jnp.bfloat16)
    total = united
    step = 512
    for n in range(0, first.shape[1], step):
        hidden = jnp.dot(normed, first[:, n : n + step], preferred_element_type=jnp.float32)
        hidden = jnp.maximum(hidden, 0.0).astype(jnp.bfloat16)
        total = total + jnp.dot(hidden, second[n : n + step, :], preferred_element_type=jnp.float32)
    return total.astype(jnp.bfloat16)


def update_kernel(far_ref, part_ref, w1_ref, w2_ref, out_ref, hub_out_ref, u_ref, u_sem, first_ref, second_ref, hidden_ref, normed_ref, w_sem, *sum_refs):
    sums_in = load_sums(far_ref, part_ref, u_ref, u_sem)
    weights = load_weights(w1_ref, w2_ref, first_ref, second_ref, w_sem, 1)
    co, core = coords()

    def to(co2, core2):
        return (device_of(co2, core2),)

    bar = pltpu.get_barrier_semaphore()
    pl.semaphore_signal(bar, inc=1, device_id=to(co, 1 - core), device_id_type=MESH)
    for dim in range(3):
        for off in (1, 2, 3):
            pl.semaphore_signal(bar, inc=1, device_id=to(moved(co, dim, off), core), device_id_type=MESH)
    pl.semaphore_wait(bar, 10)

    def remote(src, dst, ssem, rsem, dev):
        return pltpu.make_async_remote_copy(src_ref=src, dst_ref=dst, send_sem=ssem, recv_sem=rsem, device_id=dev, device_id_type=MESH)

    sums = HubSum(co, core, remote, to, u_ref, *sum_refs)
    sums_in(STEPS)
    sums.start(0)
    weights()
    size = hidden_ref.shape[0]
    for q in range(STEPS):
        sums_in(q)
        update_rows(u_ref, out_ref, q, size, first_ref, second_ref, hidden_ref, normed_ref)
        if q == 0:
            sums.wait(0)
            sums.add(0)
        if q == 1:
            sums.start(1)
        if q == 5:
            sums.wait(1)
            sums.add(1)
            sums.start(2)
    sums.wait(2)
    sums.add(2)
    sums.start(3)
    sums.wait(3)
    hub_out_ref[...] = feed_forward(sums.result(), first_ref, second_ref)


def update(u, part, w_in, w_out):
    bf = jnp.bfloat16
    V, A = pl.BlockSpec(memory_space=pltpu.VMEM), pl.BlockSpec(memory_space=pl.ANY)
    return pl.pallas_call(
        update_kernel,
        out_shape=(jax.ShapeDtypeStruct((32, 128, 256), bf), jax.ShapeDtypeStruct((16, 256), bf)),
        in_specs=[A, A, A, A],
        out_specs=(V, V),
        scratch_shapes=weight_scratch(512) + sum_scratch(),
        compiler_params=pltpu.CompilerParams(collective_id=2, has_side_effects=True, vmem_limit_bytes=60 * 2**20),
        name="update",
    )(u.reshape(192, 2, 16, 256), part.reshape(-1, 2, 16, 256), w_in, w_out)


def body(peripheral, hubs, tiles, tile_rows, local_cols, tile_count, send_list, hub_place, w_in, w_out):
    x = peripheral.reshape(-1, 128, 256)
    landed, table, near = exchange(x, send_list, hubs, hub_place)
    (u,) = sum_tiles(False, tile_rows, local_cols, tile_count, hub_place, tiles, x, table, landed)
    landed, table, x = update_exchange(u, near, w_in, w_out)
    u, part = sum_tiles(True, tile_rows, local_cols, tile_count, hub_place, tiles, x, table, landed)
    new, hub_new = update(u, part, w_in, w_out)
    return new.reshape(peripheral.shape), hub_new


def solution(mesh):
    split = P("dev")
    in_specs = (split, split, split, split, split, split, split, P(), P(), P())
    return jax.shard_map(body, mesh=mesh, in_specs=in_specs, out_specs=(split, split), check_vma=False)
```
